128 devices in a mesh: gz: 8 (over x, core), xy: 16 (over y, z).
Axes of the slice: x: 4, y: 4, z: 4, core: 2. Of those that a mesh axis runs over, the one named last changes fastest.
Arguments:
- thermal_load: float32 [128, 4, 256, 384], P('gz', None, 'xy'), may hold values from -12 to 12
- material: int32 [128, 256, 384], P('gz', 'xy'), may hold values from 0 to 7
- layer_ids: int32 [128, 256, 384], P('gz', 'xy'), may hold values from 0 to 5
- stiffness: float32 [8, 4, 4], replicated, may hold values from -0.7 to 13, as said below
- coupling: float32 [6, 4, 4], replicated, may hold values from -0.15 to 0.9, as said below
- pivots: float32 [8, 4, 4], replicated, may hold values from -0.015 to 0.14, as said below
- factor: float32 [6, 4, 4], replicated, may hold values from -0.01 to 1
Outputs:
- solution: float32 [128, 4, 256, 384], P('gz', None, 'xy')
- residual: float32 [128, 4, 256, 384], P('gz', None, 'xy')
The draws below stay inside these ranges and needn't reach their ends.
Inputs may be any that keep to these rules, and one draw needn't show every extreme that they name: `stiffness`: each block is symmetric, and the operator A of the steps is positive definite. `coupling`: each block is symmetric. `pivots`: each block is symmetric positive definite.
All inputs are finite; a program needn't handle non-finite values.
Results may differ from the reference program's by a relative error of at most 0.0003.
Values sent between devices are 32-bit elements; how exact they have to be, the bound alone decides.
No kernel may reach another device: no remote copies, remote signals or barrier semaphores. Data moves between devices by JAX's collectives and lax.ppermute only.
A program may use at most 192 MiB of HBM per device.

```python
import jax
import jax.numpy as jnp
from jax import lax

NY = 384
NMAT = 8
NLAY = 6
ITERS = 2
THICKNESS_CELLS = 128
NX = 256


def symmetric_offdiag(subkey, table_entries, spread):
    sampled = jax.random.uniform(subkey, (table_entries, 4, 4), jnp.float32, -spread, spread)
    upper_part = jnp.triu(sampled, 1)
    return upper_part + jnp.swapaxes(upper_part, 1, 2)


def with_diagonal(offdiag, diagonal_values):
    return offdiag + diagonal_values[:, :, None] * jnp.eye(4, dtype=jnp.float32)[None]


def draw_thermal_load(key, part):
    random_subkey_list = jax.random.split(key, 1)
    depth_frac = jnp.arange(THICKNESS_CELLS, dtype=jnp.float32) / max(THICKNESS_CELLS - 1, 1)
    width_frac = jnp.arange(NX, dtype=jnp.float32) / max(NX - 1, 1)
    scaling = jnp.exp(0.5 * jnp.log(3.0) * (depth_frac[:, None, None, None] + width_frac[None, None, :, None]))
    sampled = jax.random.normal(random_subkey_list[0], (THICKNESS_CELLS, 4, NX, NY), jnp.float32)
    return jnp.clip(sampled * scaling, -12.0, 12.0)


def draw_layer_ids(key, part):
    random_subkey_list = jax.random.split(key, 4)
    planes = jax.random.randint(random_subkey_list[0], (THICKNESS_CELLS,), 0, NLAY - 1)
    scattered = jax.random.randint(random_subkey_list[1], (THICKNESS_CELLS, NX, NY), 0, NLAY - 1)
    picked = jax.random.randint(random_subkey_list[2], (THICKNESS_CELLS, NX, NY), 0, 4) == 0
    labels = jnp.where(picked, scattered, planes[:, None, None])
    split_groups = jax.random.randint(random_subkey_list[3], (2,), 0, THICKNESS_CELLS)
    depth_levels = jnp.arange(THICKNESS_CELLS, dtype=jnp.int32)
    splitting_apart = jnp.any(depth_levels[:, None] == split_groups[None, :], axis=1)
    return jnp.where(splitting_apart[:, None, None], NLAY - 1, labels).astype(jnp.int32)


def draw_stiffness(key, part):
    random_subkey_list = jax.random.split(key, 2)
    diagonal_values = jax.random.uniform(random_subkey_list[1], (NMAT, 4), jnp.float32, 9.0, 13.0)
    return with_diagonal(symmetric_offdiag(random_subkey_list[0], NMAT, 0.7), diagonal_values)


def draw_coupling(key, part):
    random_subkey_list = jax.random.split(key, 2)
    diagonal_values = jax.random.uniform(random_subkey_list[1], (NLAY, 4), jnp.float32, 0.3, 0.9)
    return with_diagonal(symmetric_offdiag(random_subkey_list[0], NLAY, 0.15), diagonal_values)


def draw_pivots(key, part):
    random_subkey_list = jax.random.split(key, 2)
    diagonal_values = jax.random.uniform(random_subkey_list[1], (NMAT, 4), jnp.float32, 0.06, 0.14)
    return with_diagonal(symmetric_offdiag(random_subkey_list[0], NMAT, 0.015), diagonal_values)


def draw_factor(key, part):
    random_subkey_list = jax.random.split(key, 6)
    ordering = jax.random.permutation(random_subkey_list[0], 4)
    keeping = 2
    slow_flag = jnp.zeros((4,), jnp.float32).at[ordering[:keeping]].set(1.0)
    slow_rate = jax.random.uniform(random_subkey_list[1], (4,), jnp.float32, 0.05, 0.3) / THICKNESS_CELLS
    fast_rate = 1.0 / jax.random.uniform(random_subkey_list[2], (4,), jnp.float32, 30.0, 50.0)
    base_rate = jnp.where(slow_flag > 0.5, slow_rate, fast_rate)
    stretch = jax.random.uniform(random_subkey_list[3], (NLAY, 4), jnp.float32, 0.5, 2.0)
    diagonal_values = jnp.exp(-base_rate[None, :] * stretch)
    splitting_apart = jax.random.uniform(random_subkey_list[4], (4,), jnp.float32, 0.6, 0.85)
    diagonal_values = diagonal_values.at[NLAY - 1].multiply(splitting_apart)
    offdiag = jax.random.uniform(random_subkey_list[5], (NLAY, 4, 4), jnp.float32, -0.25, 0.25) / THICKNESS_CELLS
    offdiag = offdiag * (1.0 - jnp.eye(4, dtype=jnp.float32))[None]
    return with_diagonal(offdiag, diagonal_values)


def place_ends(drawn, own_key, least, largest):
    index_at = [jax.random.randint(jax.random.fold_in(own_key, axis), (), 0, length) for axis, length in enumerate(drawn.shape)]
    widest = drawn.shape.index(max(drawn.shape))
    beside = index_at[:widest] + [(index_at[widest] + 1) % drawn.shape[widest]] + index_at[widest + 1:]
    return drawn.at[tuple(index_at)].set(least).at[tuple(beside)].set(largest)


def setup_inputs(seed: int = 0) -> dict:
    seeds = jax.random.split(jax.random.key(seed), 8)
    thermal_load = draw_thermal_load(jax.random.fold_in(seeds[7], 71), 0)
    material = place_ends(jax.random.randint(seeds[1], (THICKNESS_CELLS, NX, NY), 0, NMAT), jax.random.fold_in(seeds[1], 1), 0, NMAT - 1).astype(jnp.int32)
    layer_ids = draw_layer_ids(jax.random.fold_in(seeds[7], 71), 0)
    stiffness = draw_stiffness(jax.random.fold_in(seeds[7], 71), 0)
    coupling = draw_coupling(jax.random.fold_in(seeds[7], 71), 0)
    pivots = draw_pivots(jax.random.fold_in(seeds[7], 71), 0)
    factor = draw_factor(jax.random.fold_in(seeds[7], 71), 0)
    return dict(thermal_load=thermal_load, material=material, layer_ids=layer_ids, stiffness=stiffness, coupling=coupling, pivots=pivots, factor=factor)


def apply_table(blocks_table, labels, vectors):
    summed = jnp.zeros_like(vectors)
    for table_row in range(blocks_table.shape[0]):
        product_rows = jnp.einsum("ij,...jxy->...ixy", blocks_table[table_row], vectors, precision=lax.Precision.HIGHEST)
        chosen = jnp.expand_dims(labels == table_row, -3)
        summed = summed + jnp.where(chosen, product_rows, jnp.zeros_like(product_rows))
    return summed


def operate(field, material, layer_ids, stiffness, coupling):
    result_rows = apply_table(stiffness, material, field)
    pushed = apply_table(coupling, layer_ids, field)
    plane_zero = jnp.zeros_like(field[:1])
    upper_field = jnp.concatenate([field[1:], plane_zero], axis=0)
    lower_pushed = jnp.concatenate([plane_zero, pushed[:-1]], axis=0)
    padded = jnp.pad(field, ((0, 0), (0, 0), (1, 1), (1, 1)))
    beside = padded[:, :, 2:, 1:-1] + padded[:, :, :-2, 1:-1]
    beside = beside + padded[:, :, 1:-1, 2:] + padded[:, :, 1:-1, :-2]
    from_upper = apply_table(coupling, layer_ids, upper_field)
    return result_rows - beside - from_upper - lower_pushed


def precondition(residual, material, layer_ids, pivots, factor):
    zeros_plane = jnp.zeros(residual.shape[1:], jnp.float32)

    def forward(carried, paired):
        plane_rows, labels = paired
        updated = plane_rows + apply_table(factor, labels, carried)
        return updated, updated

    _, climbed = lax.scan(forward, zeros_plane, (residual, layer_ids))
    scaled = apply_table(pivots, material, climbed)
    transposed = jnp.swapaxes(factor, 1, 2)

    def backward(carried, paired):
        plane_rows, labels = paired
        updated = plane_rows + carried
        return apply_table(transposed, labels, updated), updated

    _, result_rows = lax.scan(backward, zeros_plane, (scaled, layer_ids), reverse=True)
    return result_rows


def reference(thermal_load, material, layer_ids, stiffness, coupling, pivots, factor):
    solution = jnp.zeros_like(thermal_load)
    residual = thermal_load
    precond = precondition(residual, material, layer_ids, pivots, factor)
    direction = precond
    precond_dot = jnp.sum(residual * precond)
    for iteration in range(ITERS):
        applied = operate(direction, material, layer_ids, stiffness, coupling)
        step_size = precond_dot / jnp.sum(direction * applied)
        solution = solution + step_size * direction
        residual = residual - step_size * applied
        if iteration + 1 < ITERS:
            precond = precondition(residual, material, layer_ids, pivots, factor)
            following_product = jnp.sum(residual * precond)
            direction = precond + (following_product / precond_dot) * direction
            precond_dot = following_product
    return solution, residual
```

```python
import jax
import jax.numpy as jnp
from jax import lax
from jax.experimental import pallas as pl
from jax.experimental.pallas import tpu as pltpu
from jax.sharding import Mesh
from jax.sharding import PartitionSpec as P

GZ = ("gz_0", "gz_1")
XY = ("xy_0", "xy_1")
ALL = GZ + XY
F32 = jnp.float32
I32 = jnp.int32

NZ = 16
NSEG = 8
COLS = [(xi, lj) for xi in range(2) for lj in range(3)]
SYM = [(i, j) for i in range(4) for j in range(i, 4)]
SYMI = {}
for _n, (_i, _j) in enumerate(SYM):
    SYMI[(_i, _j)] = _n
    SYMI[(_j, _i)] = _n
T_P, T_S, T_K, T_C = 0, 16, 26, 36
NTAB = 46
NONE = 127
R1, R2, R3 = 224, 72, 56
MIB = 1 << 20


def tile(xi, lj):
    return pl.ds(8 * xi, 8), pl.ds(128 * lj, 128)


def look(tabs, first, count, ids):
    return [
        jnp.take_along_axis(tabs[first + e], ids, axis=1, mode="promise_in_bounds")
        for e in range(count)
    ]


def fsum(terms):
    terms = list(terms)
    while len(terms) > 1:
        terms = [
            terms[n] + terms[n + 1] if n + 1 < len(terms) else terms[n]
            for n in range(0, len(terms), 2)
        ]
    return terms[0]


def full(blk, v):
    return [fsum(blk[4 * i + j] * v[j] for j in range(4)) for i in range(4)]


def full_t(blk, v):
    return [fsum(blk[4 * i + j] * v[i] for i in range(4)) for j in range(4)]


def symm(blk, v):
    return [fsum(blk[SYMI[(i, j)]] * v[j] for j in range(4)) for i in range(4)]


def add(a, b):
    return [x + y for x, y in zip(a, b)]


def build_tables(tabs, fac, piv, stf, cpl):
    lane = lax.broadcasted_iota(I32, (8, 128), 1)
    zero = jnp.zeros((8, 128), F32)
    for src, first, count, pairs in (
        (fac, T_P, 6, [(i, j) for i in range(4) for j in range(4)]),
        (piv, T_S, 8, SYM),
        (stf, T_K, 8, SYM),
        (cpl, T_C, 6, SYM),
    ):
        for e, (i, j) in enumerate(pairs):
            row = zero
            for m in range(count):
                row = jnp.where(lane == m, src[m, i, j], row)
            tabs[first + e] = row


def first_sweep(r, mat, lay, fac, piv, stf, cpl, send, tabs):
    build_tables(tabs, fac, piv, stf, cpl)
    for n, (xi, lj) in enumerate(COLS):
        rows, lanes = tile(xi, lj)

        def level(z, state):
            g, x, q, w = state[:4], state[4:20], state[20:30], state[30:34]
            blk = look(tabs, T_P, 16, lay[z, rows, lanes])
            g = add([r[z, c, rows, lanes] for c in range(4)], full(blk, g))
            xcols = [full(blk, [x[4 * j + c] for j in range(4)]) for c in range(4)]
            piv_blk = look(tabs, T_S, 10, mat[z, rows, lanes])
            h = symm(piv_blk, g)
            w = [w[c] + fsum(xcols[c][i] * h[i] for i in range(4)) for c in range(4)]
            q = list(q)
            for c in range(4):
                sx = symm(piv_blk, xcols[c])
                for d in range(c + 1):
                    e = SYMI[(d, c)]
                    q[e] = q[e] + fsum(xcols[d][i] * sx[i] for i in range(4))
            x = [xcols[c][j] for j in range(4) for c in range(4)]
            return tuple(list(g) + x + q + list(w))

        zero = jnp.zeros((8, 128), F32)
        one = jnp.ones((8, 128), F32)
        g = [r[0, c, rows, lanes] for c in range(4)]
        q = look(tabs, T_S, 10, mat[0, rows, lanes])
        w = symm(q, g)
        x = [one if i == j else zero for i in range(4) for j in range(4)]
        state = lax.fori_loop(1, NZ, level, tuple(g + x + q + w))
        g, x, q, w = state[:4], state[4:20], state[20:30], state[30:34]
        ids = [lay[0, rows, lanes], lay[NZ - 1, rows, lanes], mat[NZ - 1, rows, lanes]]
        values = list(g) + list(w) + list(x) + list(q) + [v.astype(F32) for v in ids]
        for v, value in enumerate(values):
            send[pl.ds(6 * v + n, 8, stride=R1), :] = value


def make_owner(first):
    out_rows = R2 if first else R3

    def owner(recv, fixed, tabs, back):
        def get(ref, per, k, v):
            return ref[pl.ds(per * k + 6 * v, 8), :]

        per = R1 if first else R3

        def ident(k, v):
            return jnp.bitwise_and(get(fixed, R1, k, v).astype(I32), 127)

        zero = jnp.zeros((8, 128), F32)
        state = [zero] * 4
        inflow = []
        bottoms = []
        for k in range(NSEG):
            for c in range(4):
                back[pl.ds(out_rows * k + 6 * c, 6), :] = state[c][:6]
            bottom = look(tabs, T_P, 16, ident(k, 34))
            bottoms.append(bottom)
            a = full(bottom, state)
            inflow.append(a)
            if k < NSEG - 1:
                x = [get(fixed, R1, k, 8 + e) for e in range(16)]
                state = add([get(recv, per, k, c) for c in range(4)], full(x, a))
        b = [zero] * 4
        t = [zero] * 4
        for k in reversed(range(NSEG)):
            for c in range(4):
                back[pl.ds(out_rows * k + 24 + 6 * c, 6), :] = b[c][:6]
            if k > 0:
                q = [get(fixed, R1, k, 24 + e) for e in range(10)]
                wb = add([get(recv, per, k, 4 + c) for c in range(4)], symm(q, inflow[k]))
                if k < NSEG - 1:
                    x = [get(fixed, R1, k, 8 + e) for e in range(16)]
                    wb = add(wb, full_t(x, t))
                b = wb
                t = full_t(bottoms[k], b)
        if first:
            none = jnp.full((6, 128), float(NONE), F32)
            for k in range(NSEG):
                above = get(fixed, R1, k + 1, 34)[:6] if k + 1 < NSEG else none
                back[pl.ds(R2 * k + 48, 6), :] = above
                for e in range(2):
                    below = get(fixed, R1, k - 1, 35 + e)[:6] if k > 0 else none
                    back[pl.ds(R2 * k + 54 + 6 * e, 6), :] = below
                back[pl.ds(R2 * k + 66, 6), :] = none

    return owner


def make_apply(first):
    per = R2 if first else R3

    def apply(r, mat, lay, back, first_back, tabs, other, u, zlow, zup, elo, ehi, dots, pscr, hscr):
        acc_r = jnp.zeros((8, 128), F32)
        acc_o = jnp.zeros((8, 128), F32)
        for n, (xi, lj) in enumerate(COLS):
            rows, lanes = tile(xi, lj)

            def get(v, ref=back, p=per):
                return ref[pl.ds(6 * v + n, 8, stride=p), :]

            inflow = [get(c) for c in range(4)]
            b = [get(4 + c) for c in range(4)]
            ids = [get(8 + e, first_back, R2).astype(I32) for e in range(3)]

            def up(z, g):
                blk = look(tabs, T_P, 16, lay[z, rows, lanes])
                for e in range(16):
                    pscr[z, e] = blk[e]
                g = add([r[z, c, rows, lanes] for c in range(4)], full(blk, g))
                h = symm(look(tabs, T_S, 10, mat[z, rows, lanes]), g)
                for c in range(4):
                    hscr[z, c] = h[c]
                return tuple(g)

            lax.fori_loop(0, NZ, up, tuple(inflow))
            t = full_t(look(tabs, T_P, 16, ids[0]), b)

            def down(s, carry):
                z = NZ - 1 - s
                t, ar, ao = carry[:4], carry[4], carry[5]
                w = add([hscr[z, c] for c in range(4)], t)
                for c in range(4):
                    u[z, c, rows, lanes] = w[c]
                ar = ar + fsum(w[c] * r[z, c, rows, lanes] for c in range(4))
                if not first:
                    ao = ao + fsum(w[c] * other[z, c, rows, lanes] for c in range(4))
                t = full_t([pscr[z, e] for e in range(16)], w)
                return tuple(t) + (ar, ao)

            carry = lax.fori_loop(0, NZ, down, tuple(t) + (acc_r, acc_o))
            t, acc_r, acc_o = carry[:4], carry[4], carry[5]
            below = add(symm(look(tabs, T_S, 10, ids[2]), inflow), t)
            pushed = symm(look(tabs, T_C, 10, ids[1]), below)
            for c in range(4):
                zlow[c, rows, lanes] = pushed[c]
                zup[c, rows, lanes] = b[c]
        dots[0] = acc_r
        dots[1] = acc_o

        def edges(z, carry):
            for c in range(4):
                elo[z, pl.ds(c, 1), :] = u[z, c, pl.ds(0, 1), :]
                ehi[z, pl.ds(c, 1), :] = u[z, c, pl.ds(15, 1), :]
            return carry

        lax.fori_loop(0, NZ, edges, 0)

    return apply


def operator(u, mat, lay, zlow, zup, tabs, out, push):
    col = lax.broadcasted_iota(I32, (8, 384), 1)
    row = lax.broadcasted_iota(I32, (8, 384), 0)
    push[...] = zlow[...]

    def level(z, carry):
        for xi in range(2):
            rows = pl.ds(8 * xi, 8)
            side = []
            for c in range(4):
                here = u[z, c, rows, :]
                west = jnp.where(col == 0, 0.0, pltpu.roll(here, 1, 1))
                east = jnp.where(col == 383, 0.0, pltpu.roll(here, 383, 1))
                other = u[z, c, pl.ds(8 * (1 - xi), 8), :]
                down = pltpu.roll(here, 1, 0)
                upw = pltpu.roll(here, 7, 0)
                if xi == 0:
                    down = jnp.where(row == 0, 0.0, down)
                    upw = jnp.where(row == 7, pltpu.roll(other, 7, 0), upw)
                else:
                    down = jnp.where(row == 0, pltpu.roll(other, 1, 0), down)
                    upw = jnp.where(row == 7, 0.0, upw)
                side.append((west + east) + (down + upw))
            for lj in range(3):
                lanes = pl.ds(128 * lj, 128)
                v = [u[z, c, rows, lanes] for c in range(4)]
                nz = jnp.minimum(z + 1, NZ - 1)
                above = [
                    jnp.where(z == NZ - 1, zup[c, rows, lanes], u[nz, c, rows, lanes])
                    for c in range(4)
                ]
                kv = symm(look(tabs, T_K, 10, mat[z, rows, lanes]), v)
                cb = look(tabs, T_C, 10, lay[z, rows, lanes])
                fa = symm(cb, above)
                fb = symm(cb, v)
                for c in range(4):
                    near = side[c][:, 128 * lj : 128 * (lj + 1)]
                    out[z, c, rows, lanes] = kv[c] - near - fa[c] - push[c, rows, lanes]
                    push[c, rows, lanes] = fb[c]
        return carry

    lax.fori_loop(0, NZ, level, 0)


def with_halo(part, lo, hi, z, c, xi, lj, row):
    rows, lanes = tile(xi, lj)
    edge = (lo if xi == 0 else hi)[z, pl.ds(c, 1), lanes]
    return part[z, c, rows, lanes] - jnp.where(row == (0 if xi == 0 else 7), edge, 0.0)


def second_sweep(part, lo, hi, u, mat, lay, tabs, image, send, dots, pscr, hscr):
    row = lax.broadcasted_iota(I32, (8, 128), 0)
    zero = jnp.zeros((8, 128), F32)
    acc = zero
    for n, (xi, lj) in enumerate(COLS):
        rows, lanes = tile(xi, lj)

        def up(z, carry):
            g, acc = carry[:4], carry[4]
            blk = look(tabs, T_P, 16, lay[z, rows, lanes])
            for e in range(16):
                pscr[z, e] = blk[e]
            img = [with_halo(part, lo, hi, z, c, xi, lj, row) for c in range(4)]
            for c in range(4):
                image[z, c, rows, lanes] = img[c]
            acc = acc + fsum(img[c] * u[z, c, rows, lanes] for c in range(4))
            g = add(img, full(blk, g))
            h = symm(look(tabs, T_S, 10, mat[z, rows, lanes]), g)
            for c in range(4):
                hscr[z, c] = h[c]
            return tuple(g) + (acc,)

        carry = lax.fori_loop(0, NZ, up, (zero,) * 4 + (acc,))
        g, acc = carry[:4], carry[4]

        def down(s, w):
            z = NZ - 2 - s
            t = full_t([pscr[z + 1, e] for e in range(16)], w)
            return tuple(add([hscr[z, c] for c in range(4)], t))

        w = lax.fori_loop(0, NZ - 1, down, tuple(hscr[NZ - 1, c] for c in range(4)))
        for v, value in enumerate(list(g) + list(w)):
            send[pl.ds(6 * v + n, 8, stride=R3), :] = value
    dots[0] = acc


def last_dots(part, lo, hi, u, w, da, db, dc, y, sums):
    row = lax.broadcasted_iota(I32, (8, 128), 0)
    zero = jnp.zeros((8, 128), F32)

    def level(z, carry):
        au, aw = carry
        for xi, lj in COLS:
            rows, lanes = tile(xi, lj)
            for c in range(4):
                val = with_halo(part, lo, hi, z, c, xi, lj, row)
                y[z, c, rows, lanes] = val
                au = au + val * u[z, c, rows, lanes]
                aw = aw + val * w[z, c, rows, lanes]
        return au, aw

    au, aw = lax.fori_loop(0, NZ, level, (zero, zero))
    lane = lax.broadcasted_iota(I32, (1, 128), 1)
    line = jnp.zeros((1, 128), F32)
    for e, part_sum in enumerate((da[0], dc[0], db[0], db[1], au, aw)):
        line = jnp.where(lane == e, jnp.sum(part_sum), line)
    sums[...] = jnp.broadcast_to(line[None], sums.shape)


def combine(sums, r, u, image, w, y, sol, res):
    tot = jnp.sum(sums[...], axis=0)
    ru, ui, iw, rw, uy, wy = [tot[:, e : e + 1] for e in range(6)]
    a0 = ru / ui
    fresh = ru - a0 * (rw + ui) + a0 * a0 * iw
    beta1 = 1.0 + fresh / ru
    curv = beta1 * beta1 * ui - beta1 * a0 * (uy + iw) + a0 * a0 * wy
    a1 = fresh / curv
    s0 = jnp.broadcast_to(a0 + a1 * beta1, (8, 128))
    s1 = jnp.broadcast_to(a1 * a0, (8, 128))

    def level(z, carry):
        for xi, lj in COLS:
            rows, lanes = tile(xi, lj)
            for c in range(4):
                at = (z, c, rows, lanes)
                sol[at] = s0 * u[at] - s1 * w[at]
                res[at] = r[at] - s0 * image[at] + s1 * y[at]
        return carry

    lax.fori_loop(0, NZ, level, 0)


def call(body, out, name, smem=(), scratch=(), nargs=0, limit=24):
    vm = pl.BlockSpec(memory_space=pltpu.VMEM)
    sm = pl.BlockSpec(memory_space=pltpu.SMEM)
    return pl.pallas_call(
        body,
        out_shape=[jax.ShapeDtypeStruct(s, F32) for s in out],
        in_specs=[sm if n in smem else vm for n in range(nargs)],
        out_specs=[vm for _ in out],
        scratch_shapes=[pltpu.VMEM(s, F32) for s in scratch],
        compiler_params=pltpu.CompilerParams(vmem_limit_bytes=limit * MIB),
        name=name,
    )


FIELD = (NZ, 4, 16, 384)
EDGE = (NZ, 4, 384)
PLANE = (4, 16, 384)
TABS = (NTAB, 8, 128)
SCR = ((NZ, 16, 8, 128), (NZ, 4, 8, 128))


def exchange(buf, per):
    buf = lax.all_to_all(buf.reshape(NSEG, per, 128), GZ, 0, 0, tiled=True)
    return buf.reshape(NSEG * per, 128)


def halo(elo, ehi):
    count = lax.axis_size(XY)
    lo = lax.ppermute(ehi, XY, [(i, i + 1) for i in range(count - 1)])
    hi = lax.ppermute(elo, XY, [(i + 1, i) for i in range(count - 1)])
    return lo, hi


def apply_m(first, r, mat, lay, back, first_back, tabs, other):
    outs = (FIELD, PLANE, PLANE, EDGE, EDGE, (2, 8, 128))
    return call(make_apply(first), outs, "apply", scratch=SCR, nargs=7)(
        r, mat, lay, back, first_back, tabs, other
    )


def per_device(load, mat, lay, stf, cpl, piv, fac):
    send, tabs = call(first_sweep, ((NSEG * R1, 128), TABS), "first_sweep", smem=(3, 4, 5, 6), nargs=7)(
        load, mat, lay, fac, piv, stf, cpl
    )
    fixed = exchange(send, R1)
    (back,) = call(make_owner(True), ((NSEG * R2, 128),), "owner1", nargs=3)(fixed, fixed, tabs)
    back1 = exchange(back, R2)
    u, zlow, zup, elo, ehi, da = apply_m(True, load, mat, lay, back1, back1, tabs, load)
    lo, hi = halo(elo, ehi)
    (part,) = call(operator, (FIELD,), "operator", scratch=(PLANE,), nargs=6)(u, mat, lay, zlow, zup, tabs)
    image, send, dc = call(
        second_sweep, (FIELD, (NSEG * R3, 128), (1, 8, 128)), "second_sweep", scratch=SCR, nargs=7
    )(part, lo, hi, u, mat, lay, tabs)
    recv = exchange(send, R3)
    (back,) = call(make_owner(False), ((NSEG * R3, 128),), "owner2", nargs=3)(recv, fixed, tabs)
    back2 = exchange(back, R3)
    w, zlow, zup, elo, ehi, db = apply_m(False, image, mat, lay, back2, back1, tabs, load)
    lo, hi = halo(elo, ehi)
    (part,) = call(operator, (FIELD,), "operator", scratch=(PLANE,), nargs=6)(w, mat, lay, zlow, zup, tabs)
    y, sums = call(last_dots, (FIELD, (128, 1, 128)), "last_dots", nargs=8)(part, lo, hi, u, w, da, db, dc)
    sums = lax.all_to_all(sums, ALL, 0, 0, tiled=True)
    return tuple(call(combine, (FIELD, FIELD), "combine", nargs=6)(sums, load, u, image, w, y))


def solution(mesh):
    finer = Mesh(mesh.devices.reshape(4, 2, 4, 4), ALL)
    return jax.shard_map(
        per_device,
        mesh=finer,
        in_specs=(P(GZ, None, XY, None), P(GZ, XY, None), P(GZ, XY, None), P(), P(), P(), P()),
        out_specs=(P(GZ, None, XY, None), P(GZ, None, XY, None)),
        check_vma=False,
    )
```

```python
import jax
import jax.numpy as jnp
from jax import lax
from jax.experimental import pallas as pl
from jax.experimental.pallas import tpu as pltpu
from jax.sharding import Mesh
from jax.sharding import PartitionSpec as P

GZ = ("gz_0", "gz_1")
XY = ("xy_0", "xy_1")
ALL = GZ + XY
F32 = jnp.float32
I32 = jnp.int32

NZ = 16
NSEG = 8
COLS = [(xi, lj) for xi in range(2) for lj in range(3)]
SYM = [(i, j) for i in range(4) for j in range(i, 4)]
SYMI = {}
for _n, (_i, _j) in enumerate(SYM):
    SYMI[(_i, _j)] = _n
    SYMI[(_j, _i)] = _n
T_P, T_S, T_K, T_C = 0, 16, 26, 36
NTAB = 46
NONE = 127
R1, R2, R3 = 224, 72, 56
MIB = 1 << 20


def tile(xi, lj):
    return pl.ds(8 * xi, 8), pl.ds(128 * lj, 128)


def look(tabs, first, count, ids):
    return [
        jnp.take_along_axis(tabs[first + e], ids, axis=1, mode="promise_in_bounds")
        for e in range(count)
    ]


def fsum(terms):
    terms = list(terms)
    while len(terms) > 1:
        terms = [
            terms[n] + terms[n + 1] if n + 1 < len(terms) else terms[n]
            for n in range(0, len(terms), 2)
        ]
    return terms[0]


def full(blk, v):
    return [fsum(blk[4 * i + j] * v[j] for j in range(4)) for i in range(4)]


def full_t(blk, v):
    return [fsum(blk[4 * i + j] * v[i] for i in range(4)) for j in range(4)]


def symm(blk, v):
    return [fsum(blk[SYMI[(i, j)]] * v[j] for j in range(4)) for i in range(4)]


def add(a, b):
    return [x + y for x, y in zip(a, b)]


def build_tables(tabs, fac, piv, stf, cpl):
    lane = lax.broadcasted_iota(I32, (8, 128), 1)
    zero = jnp.zeros((8, 128), F32)
    for src, first, count, pairs in (
        (fac, T_P, 6, [(i, j) for i in range(4) for j in range(4)]),
        (piv, T_S, 8, SYM),
        (stf, T_K, 8, SYM),
        (cpl, T_C, 6, SYM),
    ):
        for e, (i, j) in enumerate(pairs):
            row = zero
            for m in range(count):
                row = jnp.where(lane == m, src[i, j, m], row)
            tabs[first + e] = row


def first_sweep(
    r_hbm, mat_hbm, lay_hbm, *refs
):
    tables, (send, tabs, r, mat, lay, st), (fac, piv, stf, cpl, sems, table_sems) = (
        refs[:4],
        refs[4:10],
        refs[10:],
    )
    loads = [
        pltpu.make_async_copy(src, dst, table_sems.at[e])
        for e, (src, dst) in enumerate(zip(tables, (fac, piv, stf, cpl)))
    ]
    for cp in loads:
        cp.start()

    def copies(z):
        return [
            pltpu.make_async_copy(src.at[z], dst.at[z], sems.at[e, z])
            for e, (src, dst) in enumerate(((r_hbm, r), (mat_hbm, mat), (lay_hbm, lay)))
        ]

    def start(z, carry):
        for cp in copies(z):
            cp.start()
        return carry

    lax.fori_loop(0, NZ, start, 0)
    for cp in loads:
        cp.wait()
    build_tables(tabs, fac, piv, stf, cpl)
    for cp in copies(0):
        cp.wait()
    zero = jnp.zeros((8, 128), F32)
    one = jnp.ones((8, 128), F32)
    G, X, Q, W = 0, 4, 20, 30
    for n, (xi, lj) in enumerate(COLS):
        rows, lanes = tile(xi, lj)
        g = [r[0, c, rows, lanes] for c in range(4)]
        q = look(tabs, T_S, 10, mat[0, rows, lanes])
        x = [one if i == c else zero for c in range(4) for i in range(4)]
        for v, value in enumerate(g + x + q + symm(q, g)):
            st[n, v] = value

    def level(z, carry):
        for cp in copies(z):
            cp.wait()
        for n, (xi, lj) in enumerate(COLS):
            rows, lanes = tile(xi, lj)
            blk = look(tabs, T_P, 16, lay[z, rows, lanes])
            g = full(blk, [st[n, G + c] for c in range(4)])
            g = add([r[z, c, rows, lanes] for c in range(4)], g)
            for c in range(4):
                st[n, G + c] = g[c]
            x = [full(blk, [st[n, X + 4 * c + i] for i in range(4)]) for c in range(4)]
            for c in range(4):
                for i in range(4):
                    st[n, X + 4 * c + i] = x[c][i]
            blk = look(tabs, T_S, 10, mat[z, rows, lanes])
            h = symm(blk, g)
            for c in range(4):
                st[n, W + c] += fsum(x[c][i] * h[i] for i in range(4))
            for c in range(4):
                sx = symm(blk, x[c])
                for d in range(c + 1):
                    st[n, Q + SYMI[(d, c)]] += fsum(x[d][i] * sx[i] for i in range(4))
        return carry

    lax.fori_loop(1, NZ, level, 0)
    for n, (xi, lj) in enumerate(COLS):
        rows, lanes = tile(xi, lj)
        values = [st[n, v] for v in (*range(4), *range(W, W + 4))]
        values += [st[n, X + 4 * j + i] for i in range(4) for j in range(4)]
        values += [st[n, Q + e] for e in range(10)]
        ids = [lay[0, rows, lanes], lay[NZ - 1, rows, lanes], mat[NZ - 1, rows, lanes]]
        for v, value in enumerate(values + [d.astype(F32) for d in ids]):
            send[pl.ds(6 * v + n, 8, stride=R1), :] = value


def make_owner(first):
    out_rows = R2 if first else R3

    def owner(recv, fixed, tabs, back):
        def get(ref, per, k, v):
            return ref[pl.ds(per * k + 6 * v, 8), :]

        per = R1 if first else R3

        def ident(k, v):
            return jnp.bitwise_and(get(fixed, R1, k, v).astype(I32), 127)

        zero = jnp.zeros((8, 128), F32)
        state = [zero] * 4
        inflow = []
        bottoms = []
        for k in range(NSEG):
            for c in range(4):
                back[pl.ds(out_rows * k + 6 * c, 6), :] = state[c][:6]
            bottom = look(tabs, T_P, 16, ident(k, 34))
            bottoms.append(bottom)
            a = full(bottom, state)
            inflow.append(a)
            if k < NSEG - 1:
                x = [get(fixed, R1, k, 8 + e) for e in range(16)]
                state = add([get(recv, per, k, c) for c in range(4)], full(x, a))
        b = [zero] * 4
        t = [zero] * 4
        for k in reversed(range(NSEG)):
            for c in range(4):
                back[pl.ds(out_rows * k + 24 + 6 * c, 6), :] = b[c][:6]
            if k > 0:
                q = [get(fixed, R1, k, 24 + e) for e in range(10)]
                wb = add([get(recv, per, k, 4 + c) for c in range(4)], symm(q, inflow[k]))
                if k < NSEG - 1:
                    x = [get(fixed, R1, k, 8 + e) for e in range(16)]
                    wb = add(wb, full_t(x, t))
                b = wb
                t = full_t(bottoms[k], b)
        if first:
            none = jnp.full((6, 128), float(NONE), F32)
            for k in range(NSEG):
                above = get(fixed, R1, k + 1, 34)[:6] if k + 1 < NSEG else none
                back[pl.ds(R2 * k + 48, 6), :] = above
                for e in range(2):
                    below = get(fixed, R1, k - 1, 35 + e)[:6] if k > 0 else none
                    back[pl.ds(R2 * k + 54 + 6 * e, 6), :] = below
                back[pl.ds(R2 * k + 66, 6), :] = none

    return owner


def make_apply(first):
    per = R2 if first else R3

    def apply(r, mat, lay, back, first_back, tabs, other, u, zlow, zup, elo, ehi, dots, pscr, hscr, st):
        def get(n, v, ref=back, p=per):
            return ref[pl.ds(6 * v + n, 8, stride=p), :]

        for n in range(6):
            for c in range(4):
                st[n, c] = get(n, c)

        def up(z, carry):
            for n, (xi, lj) in enumerate(COLS):
                rows, lanes = tile(xi, lj)
                blk = look(tabs, T_P, 16, lay[z, rows, lanes])
                for e in range(16):
                    pscr[z, n, e] = blk[e]
                g = full(blk, [st[n, c] for c in range(4)])
                g = add([r[z, c, rows, lanes] for c in range(4)], g)
                for c in range(4):
                    st[n, c] = g[c]
                h = symm(look(tabs, T_S, 10, mat[z, rows, lanes]), g)
                for c in range(4):
                    hscr[z, n, c] = h[c]
            return carry

        lax.fori_loop(0, NZ, up, 0)
        zero = jnp.zeros((8, 128), F32)
        for n, (xi, lj) in enumerate(COLS):
            rows, lanes = tile(xi, lj)
            b = [get(n, 4 + c) for c in range(4)]
            t = full_t(look(tabs, T_P, 16, get(n, 8, first_back, R2).astype(I32)), b)
            for c in range(4):
                zup[c, rows, lanes] = b[c]
                st[n, c] = t[c]

        def down(s, carry):
            z = NZ - 1 - s
            ar, ao = carry
            for n, (xi, lj) in enumerate(COLS):
                rows, lanes = tile(xi, lj)
                w = [hscr[z, n, c] + st[n, c] for c in range(4)]
                for c in range(4):
                    u[z, c, rows, lanes] = w[c]
                ar = ar + fsum(w[c] * r[z, c, rows, lanes] for c in range(4))
                if not first:
                    ao = ao + fsum(w[c] * other[z, c, rows, lanes] for c in range(4))
                t = full_t([pscr[z, n, e] for e in range(16)], w)
                for c in range(4):
                    st[n, c] = t[c]
            return ar, ao

        acc_r, acc_o = lax.fori_loop(0, NZ, down, (zero, zero))
        dots[0] = acc_r
        dots[1] = acc_o
        for n, (xi, lj) in enumerate(COLS):
            rows, lanes = tile(xi, lj)
            lay_id, mat_id = [get(n, 9 + e, first_back, R2).astype(I32) for e in range(2)]
            below = symm(look(tabs, T_S, 10, mat_id), [get(n, c) for c in range(4)])
            below = add(below, [st[n, c] for c in range(4)])
            pushed = symm(look(tabs, T_C, 10, lay_id), below)
            for c in range(4):
                zlow[c, rows, lanes] = pushed[c]

        def edges(z, carry):
            for c in range(4):
                elo[z, pl.ds(c, 1), :] = u[z, c, pl.ds(0, 1), :]
                ehi[z, pl.ds(c, 1), :] = u[z, c, pl.ds(15, 1), :]
            return carry

        lax.fori_loop(0, NZ, edges, 0)

    return apply


def operator(u, mat, lay, zlow, zup, tabs, out, push):
    col = lax.broadcasted_iota(I32, (8, 384), 1)
    row = lax.broadcasted_iota(I32, (8, 384), 0)
    push[...] = zlow[...]

    def level(z, carry):
        for xi in range(2):
            rows = pl.ds(8 * xi, 8)
            side = []
            for c in range(4):
                here = u[z, c, rows, :]
                west = jnp.where(col == 0, 0.0, pltpu.roll(here, 1, 1))
                east = jnp.where(col == 383, 0.0, pltpu.roll(here, 383, 1))
                other = u[z, c, pl.ds(8 * (1 - xi), 8), :]
                down = pltpu.roll(here, 1, 0)
                upw = pltpu.roll(here, 7, 0)
                if xi == 0:
                    down = jnp.where(row == 0, 0.0, down)
                    upw = jnp.where(row == 7, pltpu.roll(other, 7, 0), upw)
                else:
                    down = jnp.where(row == 0, pltpu.roll(other, 1, 0), down)
                    upw = jnp.where(row == 7, 0.0, upw)
                side.append((west + east) + (down + upw))
            for lj in range(3):
                lanes = pl.ds(128 * lj, 128)
                v = [u[z, c, rows, lanes] for c in range(4)]
                nz = jnp.minimum(z + 1, NZ - 1)
                above = [
                    jnp.where(z == NZ - 1, zup[c, rows, lanes], u[nz, c, rows, lanes])
                    for c in range(4)
                ]
                kv = symm(look(tabs, T_K, 10, mat[z, rows, lanes]), v)
                cb = look(tabs, T_C, 10, lay[z, rows, lanes])
                fa = symm(cb, above)
                fb = symm(cb, v)
                for c in range(4):
                    near = side[c][:, 128 * lj : 128 * (lj + 1)]
                    out[z, c, rows, lanes] = kv[c] - near - fa[c] - push[c, rows, lanes]
                    push[c, rows, lanes] = fb[c]
        return carry

    lax.fori_loop(0, NZ, level, 0)


def with_halo(part, lo, hi, z, c, xi, lj, row):
    rows, lanes = tile(xi, lj)
    edge = (lo if xi == 0 else hi)[z, pl.ds(c, 1), lanes]
    return part[z, c, rows, lanes] - jnp.where(row == (0 if xi == 0 else 7), edge, 0.0)


def second_sweep(part, lo, hi, u, mat, lay, tabs, image, send, dots, pscr, hscr, st):
    row = lax.broadcasted_iota(I32, (8, 128), 0)
    zero = jnp.zeros((8, 128), F32)
    for n in range(6):
        for c in range(4):
            st[n, c] = zero

    def up(z, acc):
        for n, (xi, lj) in enumerate(COLS):
            rows, lanes = tile(xi, lj)
            blk = look(tabs, T_P, 16, lay[z, rows, lanes])
            for e in range(16):
                pscr[z, n, e] = blk[e]
            img = [with_halo(part, lo, hi, z, c, xi, lj, row) for c in range(4)]
            for c in range(4):
                image[z, c, rows, lanes] = img[c]
            acc = acc + fsum(img[c] * u[z, c, rows, lanes] for c in range(4))
            g = add(img, full(blk, [st[n, c] for c in range(4)]))
            for c in range(4):
                st[n, c] = g[c]
            h = symm(look(tabs, T_S, 10, mat[z, rows, lanes]), g)
            for c in range(4):
                hscr[z, n, c] = h[c]
        return acc

    dots[0] = lax.fori_loop(0, NZ, up, zero)
    for n in range(6):
        for c in range(4):
            send[pl.ds(6 * c + n, 8, stride=R3), :] = st[n, c]
            st[n, c] = hscr[NZ - 1, n, c]

    def down(s, carry):
        z = NZ - 2 - s
        for n in range(6):
            t = full_t([pscr[z + 1, n, e] for e in range(16)], [st[n, c] for c in range(4)])
            for c in range(4):
                st[n, c] = hscr[z, n, c] + t[c]
        return carry

    lax.fori_loop(0, NZ - 1, down, 0)
    for n in range(6):
        for c in range(4):
            send[pl.ds(6 * (4 + c) + n, 8, stride=R3), :] = st[n, c]


def last_dots(part, lo, hi, u, w, da, db, dc, y, sums):
    row = lax.broadcasted_iota(I32, (8, 128), 0)
    zero = jnp.zeros((8, 128), F32)

    def level(z, carry):
        au, aw = carry
        for xi, lj in COLS:
            rows, lanes = tile(xi, lj)
            for c in range(4):
                val = with_halo(part, lo, hi, z, c, xi, lj, row)
                y[z, c, rows, lanes] = val
                au = au + val * u[z, c, rows, lanes]
                aw = aw + val * w[z, c, rows, lanes]
        return au, aw

    au, aw = lax.fori_loop(0, NZ, level, (zero, zero))
    lane = lax.broadcasted_iota(I32, (1, 128), 1)
    line = jnp.zeros((1, 128), F32)
    for e, part_sum in enumerate((da[0], dc[0], db[0], db[1], au, aw)):
        line = jnp.where(lane == e, jnp.sum(part_sum), line)
    sums[...] = jnp.broadcast_to(line[None], sums.shape)


def combine(sums, r, u, image, w, y, sol, res):
    tot = jnp.sum(sums[...], axis=0)
    ru, ui, iw, rw, uy, wy = [tot[:, e : e + 1] for e in range(6)]
    a0 = ru / ui
    fresh = ru - a0 * (rw + ui) + a0 * a0 * iw
    beta1 = 1.0 + fresh / ru
    curv = beta1 * beta1 * ui - beta1 * a0 * (uy + iw) + a0 * a0 * wy
    a1 = fresh / curv
    s0 = jnp.broadcast_to(a0 + a1 * beta1, (8, 128))
    s1 = jnp.broadcast_to(a1 * a0, (8, 128))

    def level(z, carry):
        for xi, lj in COLS:
            rows, lanes = tile(xi, lj)
            for c in range(4):
                at = (z, c, rows, lanes)
                sol[at] = s0 * u[at] - s1 * w[at]
                res[at] = r[at] - s0 * image[at] + s1 * y[at]
        return carry

    lax.fori_loop(0, NZ, level, 0)


def call(body, out, name, nargs, hbm=(), scratch=(), sems=(), limit=28):
    vm = pl.BlockSpec(memory_space=pltpu.VMEM)
    hb = pl.BlockSpec(memory_space=pltpu.HBM)
    return pl.pallas_call(
        body,
        out_shape=[s if hasattr(s, "dtype") else jax.ShapeDtypeStruct(s, F32) for s in out],
        in_specs=[hb if n in hbm else vm for n in range(nargs)],
        out_specs=[vm for _ in out],
        scratch_shapes=[s if hasattr(s, "dtype") else pltpu.VMEM(s, F32) for s in scratch]
        + [pltpu.SemaphoreType.DMA(s) for s in sems],
        compiler_params=pltpu.CompilerParams(vmem_limit_bytes=limit * MIB),
        name=name,
    )


FIELD = (NZ, 4, 16, 384)
EDGE = (NZ, 4, 384)
PLANE = (4, 16, 384)
TABS = (NTAB, 8, 128)
SCR = ((NZ, 6, 16, 8, 128), (NZ, 6, 4, 8, 128), (6, 4, 8, 128))
IDS = jax.ShapeDtypeStruct((NZ, 16, 384), I32)


def exchange(buf, per):
    buf = lax.all_to_all(buf.reshape(NSEG, per, 128), GZ, 0, 0, tiled=True)
    return buf.reshape(NSEG * per, 128)


def halo(elo, ehi):
    count = lax.axis_size(XY)
    lo = lax.ppermute(ehi, XY, [(i, i + 1) for i in range(count - 1)])
    hi = lax.ppermute(elo, XY, [(i + 1, i) for i in range(count - 1)])
    return lo, hi


def apply_m(first, r, mat, lay, back, first_back, tabs, other):
    outs = (FIELD, PLANE, PLANE, EDGE, EDGE, (2, 8, 128))
    return call(make_apply(first), outs, "apply", 7, scratch=SCR)(
        r, mat, lay, back, first_back, tabs, other
    )


def operate(u, mat, lay, zlow, zup, tabs):
    return call(operator, (FIELD,), "operator", 6, scratch=(PLANE,))(u, mat, lay, zlow, zup, tabs)[0]


def per_device(load, mat, lay, stf, cpl, piv, fac):
    hbm_args = [load, mat, lay] + [jnp.transpose(t, (1, 2, 0)) for t in (fac, piv, stf, cpl)]
    hbm_args = [pltpu.with_memory_space_constraint(v, pltpu.HBM) for v in hbm_args]
    send, tabs, load, mat, lay = call(
        first_sweep,
        ((NSEG * R1, 128), TABS, FIELD, IDS, IDS),
        "first_sweep",
        7,
        hbm=range(7),
        scratch=[(6, 34, 8, 128)] + [pltpu.SMEM(v.shape, F32) for v in hbm_args[3:]],
        sems=((3, NZ), (4,)),
    )(*hbm_args)
    fixed = exchange(send, R1)
    (back,) = call(make_owner(True), ((NSEG * R2, 128),), "owner1", 3)(fixed, fixed, tabs)
    back1 = exchange(back, R2)
    u, zlow, zup, elo, ehi, da = apply_m(True, load, mat, lay, back1, back1, tabs, load)
    lo, hi = halo(elo, ehi)
    part = operate(u, mat, lay, zlow, zup, tabs)
    image, send, dc = call(
        second_sweep, (FIELD, (NSEG * R3, 128), (1, 8, 128)), "second_sweep", 7, scratch=SCR
    )(part, lo, hi, u, mat, lay, tabs)
    recv = exchange(send, R3)
    (back,) = call(make_owner(False), ((NSEG * R3, 128),), "owner2", 3)(recv, fixed, tabs)
    back2 = exchange(back, R3)
    w, zlow, zup, elo, ehi, db = apply_m(False, image, mat, lay, back2, back1, tabs, load)
    lo, hi = halo(elo, ehi)
    part = operate(w, mat, lay, zlow, zup, tabs)
    y, sums = call(last_dots, (FIELD, (128, 1, 128)), "last_dots", 8)(part, lo, hi, u, w, da, db, dc)
    sums = lax.all_to_all(sums, ALL, 0, 0, tiled=True)
    return tuple(call(combine, (FIELD, FIELD), "combine", 6)(sums, load, u, image, w, y))


def solution(mesh):
    finer = Mesh(mesh.devices.reshape(4, 2, 4, 4), ALL)
    return jax.shard_map(
        per_device,
        mesh=finer,
        in_specs=(P(GZ, None, XY, None), P(GZ, XY, None), P(GZ, XY, None), P(), P(), P(), P()),
        out_specs=(P(GZ, None, XY, None), P(GZ, None, XY, None)),
        check_vma=False,
    )
```

```python
import jax
import jax.numpy as jnp
from jax import lax
from jax.experimental import pallas as pl
from jax.experimental.pallas import tpu as pltpu
from jax.sharding import Mesh
from jax.sharding import PartitionSpec as P

GZ = ("gz_0", "gz_1")
XY = ("xy_0", "xy_1")
ALL = GZ + XY
F32 = jnp.float32
I32 = jnp.int32

NZ = 16
NSEG = 4
COLS = [(xi, lj) for xi in range(2) for lj in range(3)]
SYM = [(i, j) for i in range(4) for j in range(i, 4)]
SYMI = {}
for _n, (_i, _j) in enumerate(SYM):
    SYMI[(_i, _j)] = _n
    SYMI[(_j, _i)] = _n
T_P, T_S, T_K, T_C = 0, 16, 26, 36
NTAB = 46
NONE = 127
R1, R2, R3 = 224, 72, 56
MIB = 1 << 20


def tile(xi, lj):
    return pl.ds(8 * xi, 8), pl.ds(128 * lj, 128)


def look(tabs, first, count, ids):
    return [
        jnp.take_along_axis(tabs[first + e], ids, axis=1, mode="promise_in_bounds")
        for e in range(count)
    ]


def fsum(terms):
    terms = list(terms)
    while len(terms) > 1:
        terms = [
            terms[n] + terms[n + 1] if n + 1 < len(terms) else terms[n]
            for n in range(0, len(terms), 2)
        ]
    return terms[0]


def full(blk, v):
    return [fsum(blk[4 * i + j] * v[j] for j in range(4)) for i in range(4)]


def full_t(blk, v):
    return [fsum(blk[4 * i + j] * v[i] for i in range(4)) for j in range(4)]


def symm(blk, v):
    return [fsum(blk[SYMI[(i, j)]] * v[j] for j in range(4)) for i in range(4)]


def add(a, b):
    return [x + y for x, y in zip(a, b)]


def half():
    return lax.axis_index("gz_1")


def put_rows(send, per, v, lj, value):
    send[pl.ds(6 * v + lj, 4, stride=per), :] = value[:4]
    send[pl.ds(6 * v + 3 + lj, 4, stride=per), :] = value[4:]


def get_rows(recv, per, v, lj):
    low = recv[pl.ds(6 * v + lj, 4, stride=per), :]
    high = recv[pl.ds(6 * v + 3 + lj, 4, stride=per), :]
    return jnp.concatenate([low, high], axis=0)


def build_tables(tabs, fac, piv, stf, cpl):
    lane = lax.broadcasted_iota(I32, (8, 128), 1)
    zero = jnp.zeros((8, 128), F32)
    for src, first, count, pairs in (
        (fac, T_P, 6, [(i, j) for i in range(4) for j in range(4)]),
        (piv, T_S, 8, SYM),
        (stf, T_K, 8, SYM),
        (cpl, T_C, 6, SYM),
    ):
        for e, (i, j) in enumerate(pairs):
            row = zero
            for m in range(count):
                row = jnp.where(lane == m, src[i, j, m], row)
            tabs[first + e] = row


def first_sweep(
    r_hbm, mat_hbm, lay_hbm, *refs
):
    tables, (keep, give, tabs, r, ps, kc), (mat, lay, st, fac, piv, stf, cpl, sems, table_sems) = (
        refs[:4],
        refs[4:10],
        refs[10:],
    )
    loads = [
        pltpu.make_async_copy(src, dst, table_sems.at[e])
        for e, (src, dst) in enumerate(zip(tables, (fac, piv, stf, cpl)))
    ]
    for cp in loads:
        cp.start()

    def copies(z):
        return [
            pltpu.make_async_copy(src.at[z], dst.at[z], sems.at[e, z])
            for e, (src, dst) in enumerate(((r_hbm, r), (mat_hbm, mat), (lay_hbm, lay)))
        ]

    def start(z, carry):
        for cp in copies(z):
            cp.start()
        return carry

    lax.fori_loop(0, NZ, start, 0)
    for cp in loads:
        cp.wait()
    build_tables(tabs, fac, piv, stf, cpl)
    for cp in copies(0):
        cp.wait()
    zero = jnp.zeros((8, 128), F32)
    one = jnp.ones((8, 128), F32)
    G, X, Q, W = 0, 4, 20, 30

    def spread(z, n, rows, lanes):
        lay_ids, mat_ids = lay[z, rows, lanes], mat[z, rows, lanes]
        blk, piv_blk = look(tabs, T_P, 16, lay_ids), look(tabs, T_S, 10, mat_ids)
        for e, value in enumerate(blk + piv_blk):
            ps[z, n, e] = value
        for e, value in enumerate(look(tabs, T_K, 10, mat_ids) + look(tabs, T_C, 10, lay_ids)):
            kc[z, n, e] = value
        return blk, piv_blk

    for n, (xi, lj) in enumerate(COLS):
        rows, lanes = tile(xi, lj)
        g = [r[0, c, rows, lanes] for c in range(4)]
        spread(0, n, rows, lanes)
        q = [ps[0, n, 16 + e] for e in range(10)]
        x = [one if i == c else zero for c in range(4) for i in range(4)]
        for v, value in enumerate(g + x + q + symm(q, g)):
            st[n, v] = value

    def level(z, carry):
        for cp in copies(z):
            cp.wait()
        for n, (xi, lj) in enumerate(COLS):
            rows, lanes = tile(xi, lj)
            blk, piv_blk = spread(z, n, rows, lanes)
            g = full(blk, [st[n, G + c] for c in range(4)])
            g = add([r[z, c, rows, lanes] for c in range(4)], g)
            for c in range(4):
                st[n, G + c] = g[c]
            x = [full(blk, [st[n, X + 4 * c + i] for i in range(4)]) for c in range(4)]
            for c in range(4):
                for i in range(4):
                    st[n, X + 4 * c + i] = x[c][i]
            h = symm(piv_blk, g)
            for c in range(4):
                st[n, W + c] += fsum(x[c][i] * h[i] for i in range(4))
            for c in range(4):
                sx = symm(piv_blk, x[c])
                for d in range(c + 1):
                    st[n, Q + SYMI[(d, c)]] += fsum(x[d][i] * sx[i] for i in range(4))
        return carry

    lax.fori_loop(1, NZ, level, 0)
    for core in range(2):

        @pl.when(half() == core)
        def _():
            for n, (xi, lj) in enumerate(COLS):
                rows, lanes = tile(xi, lj)
                values = [st[n, v] for v in (*range(4), *range(W, W + 4))]
                values += [st[n, X + 4 * j + i] for i in range(4) for j in range(4)]
                values += [st[n, Q + e] for e in range(10)]
                ids = [lay[0, rows, lanes], lay[NZ - 1, rows, lanes], mat[NZ - 1, rows, lanes]]
                for v, value in enumerate(values + [d.astype(F32) for d in ids]):
                    (keep if xi == core else give)[v, lj] = value


def make_merge(first):
    count, per = (37, R1) if first else (8, R3)

    def merge(*refs):
        if first:
            keep, got, tabs, lu, send = refs
            fixed = lu
        else:
            keep, got, fixed, tabs, lu, send = refs
        lower = half() == 0
        for lj in range(3):
            for v in range(count):
                mine, other = keep[v, lj], got[v, lj]
                lu[0, v, lj] = jnp.where(lower, mine, other)
                lu[1, v, lj] = jnp.where(lower, other, mine)
            bottom = look(tabs, T_P, 16, fixed[1, 34, lj].astype(I32))
            xl = [fixed[0, 8 + e, lj] for e in range(16)]
            xu = [fixed[1, 8 + e, lj] for e in range(16)]
            qu = [fixed[1, 24 + e, lj] for e in range(10)]
            y = [full(bottom, [xl[4 * i + c] for i in range(4)]) for c in range(4)]
            a = full(bottom, [lu[0, c, lj] for c in range(4)])
            o = add([lu[1, c, lj] for c in range(4)], full(xu, a))
            b = add([lu[1, 4 + c, lj] for c in range(4)], symm(qu, a))
            w = [lu[0, 4 + c, lj] + fsum(y[c][i] * b[i] for i in range(4)) for c in range(4)]
            values = o + w
            if first:
                xc = [full(xu, y[c]) for c in range(4)]
                values += [xc[j][i] for i in range(4) for j in range(4)]
                qy = [symm(qu, y[c]) for c in range(4)]
                values += [
                    fixed[0, 24 + e, lj] + fsum(y[d][i] * qy[c][i] for i in range(4))
                    for e, (d, c) in enumerate(SYM)
                ]
                values += [fixed[0, 34, lj], fixed[1, 35, lj], fixed[1, 36, lj]]
            for v, value in enumerate(values):
                put_rows(send, per, v, lj, value)

    return merge


def make_split(first):
    count, per = (11, R2) if first else (8, R3)

    def split(lu, fixed, back, first_back, tabs, keep, give):
        lower = half() == 0
        for lj in range(3):
            g0 = [get_rows(back, per, c, lj) for c in range(4)]
            b1 = [get_rows(back, per, 4 + c, lj) for c in range(4)]
            ids = [get_rows(first_back, R2, 8 + e, lj) for e in range(3)]
            a0 = full(look(tabs, T_P, 16, fixed[0, 34, lj].astype(I32)), g0)
            g1 = full([fixed[0, 8 + e, lj] for e in range(16)], a0)
            g1 = add([lu[0, c, lj] for c in range(4)], g1)
            a1 = full(look(tabs, T_P, 16, fixed[1, 34, lj].astype(I32)), g1)
            t = full_t(look(tabs, T_P, 16, ids[0].astype(I32)), b1)
            b0 = add(
                symm([fixed[1, 24 + e, lj] for e in range(10)], a1),
                full_t([fixed[1, 8 + e, lj] for e in range(16)], t),
            )
            b0 = add([lu[1, 4 + c, lj] for c in range(4)], b0)
            low = g0 + b0 + [fixed[1, 34, lj], ids[1], ids[2]]
            high = g1 + b1 + [ids[0], fixed[0, 35, lj], fixed[0, 36, lj]]
            for v in range(count):
                keep[v, lj] = jnp.where(lower, low[v], high[v])
                give[v, lj] = jnp.where(lower, high[v], low[v])

    return split


def make_owner(first):
    out_rows = R2 if first else R3

    def owner(recv, fixed, tabs, back):
        def get(ref, per, k, v):
            return ref[pl.ds(per * k + 6 * v, 8), :]

        per = R1 if first else R3

        def ident(k, v):
            return jnp.bitwise_and(get(fixed, R1, k, v).astype(I32), 127)

        zero = jnp.zeros((8, 128), F32)
        state = [zero] * 4
        inflow = []
        bottoms = []
        for k in range(NSEG):
            for c in range(4):
                back[pl.ds(out_rows * k + 6 * c, 6), :] = state[c][:6]
            bottom = look(tabs, T_P, 16, ident(k, 34))
            bottoms.append(bottom)
            a = full(bottom, state)
            inflow.append(a)
            if k < NSEG - 1:
                x = [get(fixed, R1, k, 8 + e) for e in range(16)]
                state = add([get(recv, per, k, c) for c in range(4)], full(x, a))
        b = [zero] * 4
        t = [zero] * 4
        for k in reversed(range(NSEG)):
            for c in range(4):
                back[pl.ds(out_rows * k + 24 + 6 * c, 6), :] = b[c][:6]
            if k > 0:
                q = [get(fixed, R1, k, 24 + e) for e in range(10)]
                wb = add([get(recv, per, k, 4 + c) for c in range(4)], symm(q, inflow[k]))
                if k < NSEG - 1:
                    x = [get(fixed, R1, k, 8 + e) for e in range(16)]
                    wb = add(wb, full_t(x, t))
                b = wb
                t = full_t(bottoms[k], b)
        if first:
            none = jnp.full((6, 128), float(NONE), F32)
            for k in range(NSEG):
                above = get(fixed, R1, k + 1, 34)[:6] if k + 1 < NSEG else none
                back[pl.ds(R2 * k + 48, 6), :] = above
                for e in range(2):
                    below = get(fixed, R1, k - 1, 35 + e)[:6] if k > 0 else none
                    back[pl.ds(R2 * k + 54 + 6 * e, 6), :] = below
                back[pl.ds(R2 * k + 66, 6), :] = none

    return owner


def make_apply(first):
    def apply(r, ps, keep, got, first_keep, first_got, tabs, other, u, zlow, zup, elo, ehi, dots, hscr, st):
        core = half()

        def get(n, v, own=keep, other=got):
            xi, lj = COLS[n]
            return jnp.where(core == xi, own[v, lj], other[v, lj])

        for n in range(6):
            for c in range(4):
                st[n, c] = get(n, c)

        def up(z, carry):
            for n, (xi, lj) in enumerate(COLS):
                rows, lanes = tile(xi, lj)
                g = full([ps[z, n, e] for e in range(16)], [st[n, c] for c in range(4)])
                g = add([r[z, c, rows, lanes] for c in range(4)], g)
                for c in range(4):
                    st[n, c] = g[c]
                h = symm([ps[z, n, 16 + e] for e in range(10)], g)
                for c in range(4):
                    hscr[z, n, c] = h[c]
            return carry

        lax.fori_loop(0, NZ, up, 0)
        zero = jnp.zeros((8, 128), F32)
        for n, (xi, lj) in enumerate(COLS):
            rows, lanes = tile(xi, lj)
            b = [get(n, 4 + c) for c in range(4)]
            t = full_t(look(tabs, T_P, 16, get(n, 8, first_keep, first_got).astype(I32)), b)
            for c in range(4):
                zup[c, rows, lanes] = b[c]
                st[n, c] = t[c]

        def down(s, carry):
            z = NZ - 1 - s
            ar, ao = carry
            for n, (xi, lj) in enumerate(COLS):
                rows, lanes = tile(xi, lj)
                w = [hscr[z, n, c] + st[n, c] for c in range(4)]
                for c in range(4):
                    u[z, c, rows, lanes] = w[c]
                ar = ar + fsum(w[c] * r[z, c, rows, lanes] for c in range(4))
                if not first:
                    ao = ao + fsum(w[c] * other[z, c, rows, lanes] for c in range(4))
                t = full_t([ps[z, n, e] for e in range(16)], w)
                for c in range(4):
                    st[n, c] = t[c]
            return ar, ao

        acc_r, acc_o = lax.fori_loop(0, NZ, down, (zero, zero))
        dots[0] = acc_r
        dots[1] = acc_o
        for n, (xi, lj) in enumerate(COLS):
            rows, lanes = tile(xi, lj)
            lay_id, mat_id = [get(n, 9 + e, first_keep, first_got).astype(I32) for e in range(2)]
            below = symm(look(tabs, T_S, 10, mat_id), [get(n, c) for c in range(4)])
            below = add(below, [st[n, c] for c in range(4)])
            pushed = symm(look(tabs, T_C, 10, lay_id), below)
            for c in range(4):
                zlow[c, rows, lanes] = pushed[c]

        def edges(z, carry):
            for c in range(4):
                elo[z, pl.ds(c, 1), :] = u[z, c, pl.ds(0, 1), :]
                ehi[z, pl.ds(c, 1), :] = u[z, c, pl.ds(15, 1), :]
            return carry

        lax.fori_loop(0, NZ, edges, 0)

    return apply


def operator(u, kc, zlow, zup, out, push):
    col = lax.broadcasted_iota(I32, (8, 384), 1)
    row = lax.broadcasted_iota(I32, (8, 384), 0)
    push[...] = zlow[...]

    def level(z, carry):
        for xi in range(2):
            rows = pl.ds(8 * xi, 8)
            side = []
            for c in range(4):
                here = u[z, c, rows, :]
                west = jnp.where(col == 0, 0.0, pltpu.roll(here, 1, 1))
                east = jnp.where(col == 383, 0.0, pltpu.roll(here, 383, 1))
                other = u[z, c, pl.ds(8 * (1 - xi), 8), :]
                down = pltpu.roll(here, 1, 0)
                upw = pltpu.roll(here, 7, 0)
                if xi == 0:
                    down = jnp.where(row == 0, 0.0, down)
                    upw = jnp.where(row == 7, pltpu.roll(other, 7, 0), upw)
                else:
                    down = jnp.where(row == 0, pltpu.roll(other, 1, 0), down)
                    upw = jnp.where(row == 7, 0.0, upw)
                side.append((west + east) + (down + upw))
            for lj in range(3):
                lanes = pl.ds(128 * lj, 128)
                v = [u[z, c, rows, lanes] for c in range(4)]
                nz = jnp.minimum(z + 1, NZ - 1)
                above = [
                    jnp.where(z == NZ - 1, zup[c, rows, lanes], u[nz, c, rows, lanes])
                    for c in range(4)
                ]
                n = 3 * xi + lj
                kv = symm([kc[z, n, e] for e in range(10)], v)
                cb = [kc[z, n, 10 + e] for e in range(10)]
                fa = symm(cb, above)
                fb = symm(cb, v)
                for c in range(4):
                    near = side[c][:, 128 * lj : 128 * (lj + 1)]
                    out[z, c, rows, lanes] = kv[c] - near - fa[c] - push[c, rows, lanes]
                    push[c, rows, lanes] = fb[c]
        return carry

    lax.fori_loop(0, NZ, level, 0)


def with_halo(part, lo, hi, z, c, xi, lj, row):
    rows, lanes = tile(xi, lj)
    edge = (lo if xi == 0 else hi)[z, pl.ds(c, 1), lanes]
    return part[z, c, rows, lanes] - jnp.where(row == (0 if xi == 0 else 7), edge, 0.0)


def second_sweep(part, lo, hi, u, ps, image, keep, give, dots, hscr, st):
    row = lax.broadcasted_iota(I32, (8, 128), 0)
    zero = jnp.zeros((8, 128), F32)
    for n in range(6):
        for c in range(4):
            st[n, c] = zero

    def up(z, acc):
        for n, (xi, lj) in enumerate(COLS):
            rows, lanes = tile(xi, lj)
            blk = [ps[z, n, e] for e in range(16)]
            img = [with_halo(part, lo, hi, z, c, xi, lj, row) for c in range(4)]
            for c in range(4):
                image[z, c, rows, lanes] = img[c]
            acc = acc + fsum(img[c] * u[z, c, rows, lanes] for c in range(4))
            g = add(img, full(blk, [st[n, c] for c in range(4)]))
            for c in range(4):
                st[n, c] = g[c]
            h = symm([ps[z, n, 16 + e] for e in range(10)], g)
            for c in range(4):
                hscr[z, n, c] = h[c]
        return acc

    dots[0] = lax.fori_loop(0, NZ, up, zero)
    up_last = []
    for n in range(6):
        for c in range(4):
            up_last.append(st[n, c])
            st[n, c] = hscr[NZ - 1, n, c]

    def down(s, carry):
        z = NZ - 2 - s
        for n in range(6):
            t = full_t([ps[z + 1, n, e] for e in range(16)], [st[n, c] for c in range(4)])
            for c in range(4):
                st[n, c] = hscr[z, n, c] + t[c]
        return carry

    for core in range(2):

        @pl.when(half() == core)
        def _():
            for n, (xi, lj) in enumerate(COLS):
                for c in range(4):
                    (keep if xi == core else give)[c, lj] = up_last[4 * n + c]

    lax.fori_loop(0, NZ - 1, down, 0)
    for core in range(2):

        @pl.when(half() == core)
        def _():
            for n, (xi, lj) in enumerate(COLS):
                for c in range(4):
                    (keep if xi == core else give)[4 + c, lj] = st[n, c]


def last_dots(part, lo, hi, u, w, da, db, dc, y, sums):
    row = lax.broadcasted_iota(I32, (8, 128), 0)
    zero = jnp.zeros((8, 128), F32)

    def level(z, carry):
        au, aw = carry
        for xi, lj in COLS:
            rows, lanes = tile(xi, lj)
            for c in range(4):
                val = with_halo(part, lo, hi, z, c, xi, lj, row)
                y[z, c, rows, lanes] = val
                au = au + val * u[z, c, rows, lanes]
                aw = aw + val * w[z, c, rows, lanes]
        return au, aw

    au, aw = lax.fori_loop(0, NZ, level, (zero, zero))
    lane = lax.broadcasted_iota(I32, (1, 128), 1)
    line = jnp.zeros((1, 128), F32)
    for e, part_sum in enumerate((da[0], dc[0], db[0], db[1], au, aw)):
        line = jnp.where(lane == e, jnp.sum(part_sum), line)
    sums[...] = jnp.broadcast_to(line[None], sums.shape)


def combine(sums, r, u, image, w, y, sol, res):
    tot = jnp.sum(sums[...], axis=0)
    ru, ui, iw, rw, uy, wy = [tot[:, e : e + 1] for e in range(6)]
    a0 = ru / ui
    fresh = ru - a0 * (rw + ui) + a0 * a0 * iw
    beta1 = 1.0 + fresh / ru
    curv = beta1 * beta1 * ui - beta1 * a0 * (uy + iw) + a0 * a0 * wy
    a1 = fresh / curv
    s0 = jnp.broadcast_to(a0 + a1 * beta1, (8, 128))
    s1 = jnp.broadcast_to(a1 * a0, (8, 128))

    def level(z, carry):
        for xi, lj in COLS:
            rows, lanes = tile(xi, lj)
            for c in range(4):
                at = (z, c, rows, lanes)
                sol[at] = s0 * u[at] - s1 * w[at]
                res[at] = r[at] - s0 * image[at] + s1 * y[at]
        return carry

    lax.fori_loop(0, NZ, level, 0)


def call(body, out, name, nargs, hbm=(), scratch=(), sems=(), limit=10):
    vm = pl.BlockSpec(memory_space=pltpu.VMEM)
    hb = pl.BlockSpec(memory_space=pltpu.HBM)
    return pl.pallas_call(
        body,
        out_shape=[s if hasattr(s, "dtype") else jax.ShapeDtypeStruct(s, F32) for s in out],
        in_specs=[hb if n in hbm else vm for n in range(nargs)],
        out_specs=[vm for _ in out],
        scratch_shapes=[s if hasattr(s, "dtype") else pltpu.VMEM(s, F32) for s in scratch]
        + [pltpu.SemaphoreType.DMA(s) for s in sems],
        compiler_params=pltpu.CompilerParams(vmem_limit_bytes=limit * MIB),
        name=name,
    )


FIELD = (NZ, 4, 16, 384)
EDGE = (NZ, 4, 384)
PLANE = (4, 16, 384)
TABS = (NTAB, 8, 128)
SCR = ((NZ, 6, 4, 8, 128), (6, 4, 8, 128))
PS = (NZ, 6, 26, 8, 128)
KC = (NZ, 6, 20, 8, 128)


def exchange(buf, per):
    buf = lax.all_to_all(buf.reshape(NSEG, per, 128), "gz_0", 0, 0, tiled=True)
    return buf.reshape(NSEG * per, 128)


def swap(buf):
    return lax.ppermute(buf, "gz_1", [(0, 1), (1, 0)])


def part_of(count):
    return (count, 3, 8, 128)


def halo(elo, ehi):
    count = lax.axis_size(XY)
    lo = lax.ppermute(ehi, XY, [(i, i + 1) for i in range(count - 1)])
    hi = lax.ppermute(elo, XY, [(i + 1, i) for i in range(count - 1)])
    return lo, hi


def apply_m(first, r, ps, inflow, first_inflow, tabs, other):
    outs = (FIELD, PLANE, PLANE, EDGE, EDGE, (2, 8, 128))
    return call(make_apply(first), outs, "apply", 8, scratch=SCR)(
        r, ps, *inflow, *first_inflow, tabs, other
    )


def operate(u, kc, zlow, zup):
    return call(operator, (FIELD,), "operator", 4, scratch=(PLANE,))(u, kc, zlow, zup)[0]


def per_device(load, mat, lay, stf, cpl, piv, fac):
    hbm_args = [load, mat, lay] + [jnp.transpose(t, (1, 2, 0)) for t in (fac, piv, stf, cpl)]
    hbm_args = [pltpu.with_memory_space_constraint(v, pltpu.HBM) for v in hbm_args]
    keep, give, tabs, load, ps, kc = call(
        first_sweep,
        (part_of(37), part_of(37), TABS, FIELD, PS, KC),
        "first_sweep",
        7,
        hbm=range(7),
        scratch=[pltpu.VMEM(mat.shape, I32), pltpu.VMEM(lay.shape, I32), (6, 34, 8, 128)]
        + [pltpu.SMEM(v.shape, F32) for v in hbm_args[3:]],
        sems=((3, NZ), (4,)),
    )(*hbm_args)
    lu, send = call(make_merge(True), ((2, *part_of(37)), (NSEG * R1, 128)), "merge1", 3)(
        keep, swap(give), tabs
    )
    fixed = exchange(send, R1)
    (back,) = call(make_owner(True), ((NSEG * R2, 128),), "owner1", 3)(fixed, fixed, tabs)
    back1 = exchange(back, R2)
    keep, give = call(make_split(True), (part_of(11),) * 2, "split1", 5)(lu, lu, back1, back1, tabs)
    inflow1 = (keep, swap(give))
    u, zlow, zup, elo, ehi, da = apply_m(True, load, ps, inflow1, inflow1, tabs, load)
    lo, hi = halo(elo, ehi)
    part = operate(u, kc, zlow, zup)
    image, keep, give, dc = call(
        second_sweep, (FIELD, part_of(8), part_of(8), (1, 8, 128)), "second_sweep", 5, scratch=SCR
    )(part, lo, hi, u, ps)
    lu2, send = call(make_merge(False), ((2, *part_of(8)), (NSEG * R3, 128)), "merge2", 4)(
        keep, swap(give), lu, tabs
    )
    recv = exchange(send, R3)
    (back,) = call(make_owner(False), ((NSEG * R3, 128),), "owner2", 3)(recv, fixed, tabs)
    back2 = exchange(back, R3)
    keep, give = call(make_split(False), (part_of(8),) * 2, "split2", 5)(lu2, lu, back2, back1, tabs)
    w, zlow, zup, elo, ehi, db = apply_m(False, image, ps, (keep, swap(give)), inflow1, tabs, load)
    lo, hi = halo(elo, ehi)
    part = operate(w, kc, zlow, zup)
    y, sums = call(last_dots, (FIELD, (128, 1, 128)), "last_dots", 8)(part, lo, hi, u, w, da, db, dc)
    sums = lax.all_to_all(sums, ALL, 0, 0, tiled=True)
    return tuple(call(combine, (FIELD, FIELD), "combine", 6)(sums, load, u, image, w, y))


def solution(mesh):
    finer = Mesh(mesh.devices.reshape(4, 2, 4, 4), ALL)
    return jax.shard_map(
        per_device,
        mesh=finer,
        in_specs=(P(GZ, None, XY, None), P(GZ, XY, None), P(GZ, XY, None), P(), P(), P(), P()),
        out_specs=(P(GZ, None, XY, None), P(GZ, None, XY, None)),
        check_vma=False,
    )
```

```python
import jax
import jax.numpy as jnp
from jax import lax
from jax.experimental import pallas as pl
from jax.experimental.pallas import tpu as pltpu
from jax.sharding import Mesh
from jax.sharding import PartitionSpec as P

GZ = ("gz_0", "gz_1")
XY = ("xy_0", "xy_1")
ALL = GZ + XY
F32 = jnp.float32
I32 = jnp.int32

NZ = 16
NSEG = 4
COLS = [(xi, lj) for xi in range(2) for lj in range(3)]
SYM = [(i, j) for i in range(4) for j in range(i, 4)]
SYMI = {}
for _n, (_i, _j) in enumerate(SYM):
    SYMI[(_i, _j)] = _n
    SYMI[(_j, _i)] = _n
T_P, T_S, T_K, T_C = 0, 16, 26, 36
NTAB = 46
NONE = 127
R1, R2, R3 = 224, 72, 56
MIB = 1 << 20


def tile(xi, lj):
    return pl.ds(8 * xi, 8), pl.ds(128 * lj, 128)


def look(tabs, first, count, ids):
    return [
        jnp.take_along_axis(tabs[first + e], ids, axis=1, mode="promise_in_bounds")
        for e in range(count)
    ]


def fsum(terms):
    terms = list(terms)
    while len(terms) > 1:
        terms = [
            terms[n] + terms[n + 1] if n + 1 < len(terms) else terms[n]
            for n in range(0, len(terms), 2)
        ]
    return terms[0]


def full(blk, v):
    return [fsum(blk[4 * i + j] * v[j] for j in range(4)) for i in range(4)]


def full_t(blk, v):
    return [fsum(blk[4 * i + j] * v[i] for i in range(4)) for j in range(4)]


def symm(blk, v):
    return [fsum(blk[SYMI[(i, j)]] * v[j] for j in range(4)) for i in range(4)]


def add(a, b):
    return [x + y for x, y in zip(a, b)]


def half():
    return lax.axis_index("gz_1")


def xy_index():
    return lax.axis_size("xy_1") * lax.axis_index("xy_0") + lax.axis_index("xy_1")


def block(chip, per):
    return pl.ds(pl.multiple_of(chip * per, 8), per)


def to_partners(blocks, outs, per):
    me = lax.axis_index("gz_0")
    for d, out in enumerate(outs):
        out[...] = blocks[block(jnp.bitwise_xor(me, d), per), :]


def from_partners(parts, blocks, per):
    me = lax.axis_index("gz_0")
    for d, part in enumerate(parts):
        blocks[block(jnp.bitwise_xor(me, d), per), :] = part[...]


def put_rows(send, per, v, lj, value):
    send[pl.ds(6 * v + lj, 4, stride=per), :] = value[:4]
    send[pl.ds(6 * v + 3 + lj, 4, stride=per), :] = value[4:]


def get_rows(recv, per, v, lj):
    low = recv[pl.ds(6 * v + lj, 4, stride=per), :]
    high = recv[pl.ds(6 * v + 3 + lj, 4, stride=per), :]
    return jnp.concatenate([low, high], axis=0)


def build_tables(tabs, fac, piv, stf, cpl):
    lane = lax.broadcasted_iota(I32, (8, 128), 1)
    zero = jnp.zeros((8, 128), F32)
    for src, first, count, pairs in (
        (fac, T_P, 6, [(i, j) for i in range(4) for j in range(4)]),
        (piv, T_S, 8, SYM),
        (stf, T_K, 8, SYM),
        (cpl, T_C, 6, SYM),
    ):
        for e, (i, j) in enumerate(pairs):
            row = zero
            for m in range(count):
                row = jnp.where(lane == m, src[i, j, m], row)
            tabs[first + e] = row


def first_sweep(
    r_hbm, mat_hbm, lay_hbm, *refs
):
    tables, (keep, give, tabs, r, ps, kc), (mat, lay, st, fac, piv, stf, cpl, sems, table_sems) = (
        refs[:4],
        refs[4:10],
        refs[10:],
    )
    loads = [
        pltpu.make_async_copy(src, dst, table_sems.at[e])
        for e, (src, dst) in enumerate(zip(tables, (fac, piv, stf, cpl)))
    ]
    for cp in loads:
        cp.start()

    def copies(z):
        return [
            pltpu.make_async_copy(src.at[z], dst.at[z], sems.at[e, z])
            for e, (src, dst) in enumerate(((r_hbm, r), (mat_hbm, mat), (lay_hbm, lay)))
        ]

    def start(z, carry):
        for cp in copies(z):
            cp.start()
        return carry

    lax.fori_loop(0, NZ, start, 0)
    for cp in loads:
        cp.wait()
    build_tables(tabs, fac, piv, stf, cpl)
    for cp in copies(0):
        cp.wait()
    zero = jnp.zeros((8, 128), F32)
    one = jnp.ones((8, 128), F32)
    G, X, Q, W = 0, 4, 20, 30

    def spread(z, n, rows, lanes):
        lay_ids, mat_ids = lay[z, rows, lanes], mat[z, rows, lanes]
        blk, piv_blk = look(tabs, T_P, 16, lay_ids), look(tabs, T_S, 10, mat_ids)
        for e, value in enumerate(blk + piv_blk):
            ps[z, n, e] = value
        for e, value in enumerate(look(tabs, T_K, 10, mat_ids) + look(tabs, T_C, 10, lay_ids)):
            kc[z, n, e] = value
        return blk, piv_blk

    for n, (xi, lj) in enumerate(COLS):
        rows, lanes = tile(xi, lj)
        g = [r[0, c, rows, lanes] for c in range(4)]
        spread(0, n, rows, lanes)
        q = [ps[0, n, 16 + e] for e in range(10)]
        x = [one if i == c else zero for c in range(4) for i in range(4)]
        for v, value in enumerate(g + x + q + symm(q, g)):
            st[n, v] = value

    def level(z, carry):
        for cp in copies(z):
            cp.wait()
        for n, (xi, lj) in enumerate(COLS):
            rows, lanes = tile(xi, lj)
            blk, piv_blk = spread(z, n, rows, lanes)
            g = full(blk, [st[n, G + c] for c in range(4)])
            g = add([r[z, c, rows, lanes] for c in range(4)], g)
            for c in range(4):
                st[n, G + c] = g[c]
            x = [full(blk, [st[n, X + 4 * c + i] for i in range(4)]) for c in range(4)]
            for c in range(4):
                for i in range(4):
                    st[n, X + 4 * c + i] = x[c][i]
            h = symm(piv_blk, g)
            for c in range(4):
                st[n, W + c] += fsum(x[c][i] * h[i] for i in range(4))
            for c in range(4):
                sx = symm(piv_blk, x[c])
                for d in range(c + 1):
                    st[n, Q + SYMI[(d, c)]] += fsum(x[d][i] * sx[i] for i in range(4))
        return carry

    lax.fori_loop(1, NZ, level, 0)
    for core in range(2):

        @pl.when(half() == core)
        def _():
            for n, (xi, lj) in enumerate(COLS):
                rows, lanes = tile(xi, lj)
                values = [st[n, v] for v in (*range(4), *range(W, W + 4))]
                values += [st[n, X + 4 * j + i] for i in range(4) for j in range(4)]
                values += [st[n, Q + e] for e in range(10)]
                ids = [lay[0, rows, lanes], lay[NZ - 1, rows, lanes], mat[NZ - 1, rows, lanes]]
                for v, value in enumerate(values + [d.astype(F32) for d in ids]):
                    (keep if xi == core else give)[v, lj] = value


def make_merge(first):
    count, per = (37, R1) if first else (8, R3)

    def merge(*refs):
        send = refs[-1]
        if first:
            keep, got, tabs, lu, *outs = refs[:-1]
            fixed = lu
        else:
            keep, got, fixed, tabs, lu, *outs = refs[:-1]
        lower = half() == 0
        for lj in range(3):
            for v in range(count):
                mine, other = keep[v, lj], got[v, lj]
                lu[0, v, lj] = jnp.where(lower, mine, other)
                lu[1, v, lj] = jnp.where(lower, other, mine)
            bottom = look(tabs, T_P, 16, fixed[1, 34, lj].astype(I32))
            xl = [fixed[0, 8 + e, lj] for e in range(16)]
            xu = [fixed[1, 8 + e, lj] for e in range(16)]
            qu = [fixed[1, 24 + e, lj] for e in range(10)]
            y = [full(bottom, [xl[4 * i + c] for i in range(4)]) for c in range(4)]
            a = full(bottom, [lu[0, c, lj] for c in range(4)])
            o = add([lu[1, c, lj] for c in range(4)], full(xu, a))
            b = add([lu[1, 4 + c, lj] for c in range(4)], symm(qu, a))
            w = [lu[0, 4 + c, lj] + fsum(y[c][i] * b[i] for i in range(4)) for c in range(4)]
            values = o + w
            if first:
                xc = [full(xu, y[c]) for c in range(4)]
                values += [xc[j][i] for i in range(4) for j in range(4)]
                qy = [symm(qu, y[c]) for c in range(4)]
                values += [
                    fixed[0, 24 + e, lj] + fsum(y[d][i] * qy[c][i] for i in range(4))
                    for e, (d, c) in enumerate(SYM)
                ]
                values += [fixed[0, 34, lj], fixed[1, 35, lj], fixed[1, 36, lj]]
            for v, value in enumerate(values):
                put_rows(send, per, v, lj, value)
        to_partners(send, outs, per)

    return merge


def make_split(first):
    count, per = (11, R2) if first else (8, R3)

    def split(*refs):
        parts = refs[:NSEG]
        if first:
            lu, tabs, keep, give, back = refs[NSEG:]
            fixed, first_back = lu, back
        else:
            lu, fixed, first_back, tabs, keep, give, back = refs[NSEG:]
        from_partners(parts, back, per)
        lower = half() == 0
        for lj in range(3):
            g0 = [get_rows(back, per, c, lj) for c in range(4)]
            b1 = [get_rows(back, per, 4 + c, lj) for c in range(4)]
            ids = [get_rows(first_back, R2, 8 + e, lj) for e in range(3)]
            a0 = full(look(tabs, T_P, 16, fixed[0, 34, lj].astype(I32)), g0)
            g1 = full([fixed[0, 8 + e, lj] for e in range(16)], a0)
            g1 = add([lu[0, c, lj] for c in range(4)], g1)
            a1 = full(look(tabs, T_P, 16, fixed[1, 34, lj].astype(I32)), g1)
            t = full_t(look(tabs, T_P, 16, ids[0].astype(I32)), b1)
            b0 = add(
                symm([fixed[1, 24 + e, lj] for e in range(10)], a1),
                full_t([fixed[1, 8 + e, lj] for e in range(16)], t),
            )
            b0 = add([lu[1, 4 + c, lj] for c in range(4)], b0)
            low = g0 + b0 + [fixed[1, 34, lj], ids[1], ids[2]]
            high = g1 + b1 + [ids[0], fixed[0, 35, lj], fixed[0, 36, lj]]
            for v in range(count):
                keep[v, lj] = jnp.where(lower, low[v], high[v])
                give[v, lj] = jnp.where(lower, high[v], low[v])

    return split


def make_owner(first):
    out_rows = R2 if first else R3

    def owner(*refs):
        parts, back = refs[:NSEG], refs[-1]
        if first:
            tabs, recv, *outs = refs[NSEG:-1]
            fixed = recv
        else:
            fixed, tabs, *outs = refs[NSEG:-2]
            recv = refs[-2]
        from_partners(parts, recv, R1 if first else R3)

        def get(ref, per, k, v):
            return ref[pl.ds(per * k + 6 * v, 8), :]

        per = R1 if first else R3

        def ident(k, v):
            return jnp.bitwise_and(get(fixed, R1, k, v).astype(I32), 127)

        zero = jnp.zeros((8, 128), F32)
        state = [zero] * 4
        inflow = []
        bottoms = []
        for k in range(NSEG):
            for c in range(4):
                back[pl.ds(out_rows * k + 6 * c, 6), :] = state[c][:6]
            bottom = look(tabs, T_P, 16, ident(k, 34))
            bottoms.append(bottom)
            a = full(bottom, state)
            inflow.append(a)
            if k < NSEG - 1:
                x = [get(fixed, R1, k, 8 + e) for e in range(16)]
                state = add([get(recv, per, k, c) for c in range(4)], full(x, a))
        b = [zero] * 4
        t = [zero] * 4
        for k in reversed(range(NSEG)):
            for c in range(4):
                back[pl.ds(out_rows * k + 24 + 6 * c, 6), :] = b[c][:6]
            if k > 0:
                q = [get(fixed, R1, k, 24 + e) for e in range(10)]
                wb = add([get(recv, per, k, 4 + c) for c in range(4)], symm(q, inflow[k]))
                if k < NSEG - 1:
                    x = [get(fixed, R1, k, 8 + e) for e in range(16)]
                    wb = add(wb, full_t(x, t))
                b = wb
                t = full_t(bottoms[k], b)
        if first:
            none = jnp.full((6, 128), float(NONE), F32)
            for k in range(NSEG):
                above = get(fixed, R1, k + 1, 34)[:6] if k + 1 < NSEG else none
                back[pl.ds(R2 * k + 48, 6), :] = above
                for e in range(2):
                    below = get(fixed, R1, k - 1, 35 + e)[:6] if k > 0 else none
                    back[pl.ds(R2 * k + 54 + 6 * e, 6), :] = below
                back[pl.ds(R2 * k + 66, 6), :] = none
        to_partners(back, outs, out_rows)

    return owner


def make_apply(first):
    def apply(r, ps, keep, got, first_keep, first_got, tabs, other, u, zlow, zup, near, far, dots, hscr, st):
        core = half()

        def get(n, v, own=keep, other=got):
            xi, lj = COLS[n]
            return jnp.where(core == xi, own[v, lj], other[v, lj])

        for n in range(6):
            for c in range(4):
                st[n, c] = get(n, c)

        def up(z, carry):
            for n, (xi, lj) in enumerate(COLS):
                rows, lanes = tile(xi, lj)
                g = full([ps[z, n, e] for e in range(16)], [st[n, c] for c in range(4)])
                g = add([r[z, c, rows, lanes] for c in range(4)], g)
                for c in range(4):
                    st[n, c] = g[c]
                h = symm([ps[z, n, 16 + e] for e in range(10)], g)
                for c in range(4):
                    hscr[z, n, c] = h[c]
            return carry

        lax.fori_loop(0, NZ, up, 0)
        zero = jnp.zeros((8, 128), F32)
        for n, (xi, lj) in enumerate(COLS):
            rows, lanes = tile(xi, lj)
            b = [get(n, 4 + c) for c in range(4)]
            t = full_t(look(tabs, T_P, 16, get(n, 8, first_keep, first_got).astype(I32)), b)
            for c in range(4):
                zup[c, rows, lanes] = b[c]
                st[n, c] = t[c]

        def down(s, carry):
            z = NZ - 1 - s
            ar, ao = carry
            for n, (xi, lj) in enumerate(COLS):
                rows, lanes = tile(xi, lj)
                w = [hscr[z, n, c] + st[n, c] for c in range(4)]
                for c in range(4):
                    u[z, c, rows, lanes] = w[c]
                ar = ar + fsum(w[c] * r[z, c, rows, lanes] for c in range(4))
                if not first:
                    ao = ao + fsum(w[c] * other[z, c, rows, lanes] for c in range(4))
                t = full_t([ps[z, n, e] for e in range(16)], w)
                for c in range(4):
                    st[n, c] = t[c]
            return ar, ao

        acc_r, acc_o = lax.fori_loop(0, NZ, down, (zero, zero))
        dots[0] = acc_r
        dots[1] = acc_o
        for n, (xi, lj) in enumerate(COLS):
            rows, lanes = tile(xi, lj)
            lay_id, mat_id = [get(n, 9 + e, first_keep, first_got).astype(I32) for e in range(2)]
            below = symm(look(tabs, T_S, 10, mat_id), [get(n, c) for c in range(4)])
            below = add(below, [st[n, c] for c in range(4)])
            pushed = symm(look(tabs, T_C, 10, lay_id), below)
            for c in range(4):
                zlow[c, rows, lanes] = pushed[c]

        even = xy_index() % 2 == 0

        def edges(z, carry):
            for c in range(4):
                first_row, last_row = u[z, c, pl.ds(0, 1), :], u[z, c, pl.ds(15, 1), :]
                near[z, pl.ds(c, 1), :] = jnp.where(even, last_row, first_row)
                far[z, pl.ds(c, 1), :] = jnp.where(even, first_row, last_row)
            return carry

        lax.fori_loop(0, NZ, edges, 0)

    return apply


def operator(u, kc, zlow, zup, out, push):
    col = lax.broadcasted_iota(I32, (8, 384), 1)
    row = lax.broadcasted_iota(I32, (8, 384), 0)
    push[...] = zlow[...]

    def level(z, carry):
        for xi in range(2):
            rows = pl.ds(8 * xi, 8)
            side = []
            for c in range(4):
                here = u[z, c, rows, :]
                west = jnp.where(col == 0, 0.0, pltpu.roll(here, 1, 1))
                east = jnp.where(col == 383, 0.0, pltpu.roll(here, 383, 1))
                other = u[z, c, pl.ds(8 * (1 - xi), 8), :]
                down = pltpu.roll(here, 1, 0)
                upw = pltpu.roll(here, 7, 0)
                if xi == 0:
                    down = jnp.where(row == 0, 0.0, down)
                    upw = jnp.where(row == 7, pltpu.roll(other, 7, 0), upw)
                else:
                    down = jnp.where(row == 0, pltpu.roll(other, 1, 0), down)
                    upw = jnp.where(row == 7, 0.0, upw)
                side.append((west + east) + (down + upw))
            for lj in range(3):
                lanes = pl.ds(128 * lj, 128)
                v = [u[z, c, rows, lanes] for c in range(4)]
                nz = jnp.minimum(z + 1, NZ - 1)
                above = [
                    jnp.where(z == NZ - 1, zup[c, rows, lanes], u[nz, c, rows, lanes])
                    for c in range(4)
                ]
                n = 3 * xi + lj
                kv = symm([kc[z, n, e] for e in range(10)], v)
                cb = [kc[z, n, 10 + e] for e in range(10)]
                fa = symm(cb, above)
                fb = symm(cb, v)
                for c in range(4):
                    near = side[c][:, 128 * lj : 128 * (lj + 1)]
                    out[z, c, rows, lanes] = kv[c] - near - fa[c] - push[c, rows, lanes]
                    push[c, rows, lanes] = fb[c]
        return carry

    lax.fori_loop(0, NZ, level, 0)


def halo_masks():
    row = lax.broadcasted_iota(I32, (8, 128), 0)
    index = xy_index()
    last = lax.axis_size("xy_0") * lax.axis_size("xy_1") - 1
    return index % 2 == 0, ((row == 0) & (index > 0), (row == 7) & (index < last))


def with_halo(part, near, far, z, c, xi, lj, masks):
    rows, lanes = tile(xi, lj)
    even, inside = masks
    a, b = near[z, pl.ds(c, 1), lanes], far[z, pl.ds(c, 1), lanes]
    edge = jnp.where(even, b, a) if xi == 0 else jnp.where(even, a, b)
    return part[z, c, rows, lanes] - jnp.where(inside[xi], edge, 0.0)


def second_sweep(part, near, far, u, ps, image, keep, give, dots, hscr, st):
    masks = halo_masks()
    zero = jnp.zeros((8, 128), F32)
    for n in range(6):
        for c in range(4):
            st[n, c] = zero

    def up(z, acc):
        for n, (xi, lj) in enumerate(COLS):
            rows, lanes = tile(xi, lj)
            blk = [ps[z, n, e] for e in range(16)]
            img = [with_halo(part, near, far, z, c, xi, lj, masks) for c in range(4)]
            for c in range(4):
                image[z, c, rows, lanes] = img[c]
            acc = acc + fsum(img[c] * u[z, c, rows, lanes] for c in range(4))
            g = add(img, full(blk, [st[n, c] for c in range(4)]))
            for c in range(4):
                st[n, c] = g[c]
            h = symm([ps[z, n, 16 + e] for e in range(10)], g)
            for c in range(4):
                hscr[z, n, c] = h[c]
        return acc

    dots[0] = lax.fori_loop(0, NZ, up, zero)
    up_last = []
    for n in range(6):
        for c in range(4):
            up_last.append(st[n, c])
            st[n, c] = hscr[NZ - 1, n, c]

    def down(s, carry):
        z = NZ - 2 - s
        for n in range(6):
            t = full_t([ps[z + 1, n, e] for e in range(16)], [st[n, c] for c in range(4)])
            for c in range(4):
                st[n, c] = hscr[z, n, c] + t[c]
        return carry

    for core in range(2):

        @pl.when(half() == core)
        def _():
            for n, (xi, lj) in enumerate(COLS):
                for c in range(4):
                    (keep if xi == core else give)[c, lj] = up_last[4 * n + c]

    lax.fori_loop(0, NZ - 1, down, 0)
    for core in range(2):

        @pl.when(half() == core)
        def _():
            for n, (xi, lj) in enumerate(COLS):
                for c in range(4):
                    (keep if xi == core else give)[4 + c, lj] = st[n, c]


def last_dots(part, near, far, u, w, da, db, dc, y, sums):
    masks = halo_masks()
    zero = jnp.zeros((8, 128), F32)

    def level(z, carry):
        au, aw = carry
        for xi, lj in COLS:
            rows, lanes = tile(xi, lj)
            for c in range(4):
                val = with_halo(part, near, far, z, c, xi, lj, masks)
                y[z, c, rows, lanes] = val
                au = au + val * u[z, c, rows, lanes]
                aw = aw + val * w[z, c, rows, lanes]
        return au, aw

    au, aw = lax.fori_loop(0, NZ, level, (zero, zero))
    lane = lax.broadcasted_iota(I32, (1, 128), 1)
    line = jnp.zeros((1, 128), F32)
    for e, part_sum in enumerate((da[0], dc[0], db[0], db[1], au, aw)):
        line = jnp.where(lane == e, jnp.sum(part_sum), line)
    sums[...] = jnp.broadcast_to(line[None], sums.shape)


def combine(sums, r, u, image, w, y, sol, res):
    tot = jnp.sum(sums[...], axis=0)
    ru, ui, iw, rw, uy, wy = [tot[:, e : e + 1] for e in range(6)]
    a0 = ru / ui
    fresh = ru - a0 * (rw + ui) + a0 * a0 * iw
    beta1 = 1.0 + fresh / ru
    curv = beta1 * beta1 * ui - beta1 * a0 * (uy + iw) + a0 * a0 * wy
    a1 = fresh / curv
    s0 = jnp.broadcast_to(a0 + a1 * beta1, (8, 128))
    s1 = jnp.broadcast_to(a1 * a0, (8, 128))

    def level(z, carry):
        for xi, lj in COLS:
            rows, lanes = tile(xi, lj)
            for c in range(4):
                at = (z, c, rows, lanes)
                sol[at] = s0 * u[at] - s1 * w[at]
                res[at] = r[at] - s0 * image[at] + s1 * y[at]
        return carry

    lax.fori_loop(0, NZ, level, 0)


def call(body, out, name, nargs, hbm=(), scratch=(), sems=(), limit=10):
    vm = pl.BlockSpec(memory_space=pltpu.VMEM)
    hb = pl.BlockSpec(memory_space=pltpu.HBM)
    return pl.pallas_call(
        body,
        out_shape=[s if hasattr(s, "dtype") else jax.ShapeDtypeStruct(s, F32) for s in out],
        in_specs=[hb if n in hbm else vm for n in range(nargs)],
        out_specs=[vm for _ in out],
        scratch_shapes=[s if hasattr(s, "dtype") else pltpu.VMEM(s, F32) for s in scratch]
        + [pltpu.SemaphoreType.DMA(s) for s in sems],
        compiler_params=pltpu.CompilerParams(vmem_limit_bytes=limit * MIB),
        name=name,
    )


FIELD = (NZ, 4, 16, 384)
EDGE = (NZ, 4, 384)
PLANE = (4, 16, 384)
TABS = (NTAB, 8, 128)
SCR = ((NZ, 6, 4, 8, 128), (6, 4, 8, 128))
PS = (NZ, 6, 26, 8, 128)
KC = (NZ, 6, 20, 8, 128)


def exchange(parts):
    count = lax.axis_size("gz_0")
    moved = [
        lax.ppermute(part, "gz_0", [(i, i ^ d) for i in range(count)])
        for d, part in enumerate(parts)
        if d > 0
    ]
    return [parts[0]] + moved


def blocks_of(per):
    return [(per, 128)] * NSEG


def swap(buf):
    return lax.ppermute(buf, "gz_1", [(0, 1), (1, 0)])


def part_of(count):
    return (count, 3, 8, 128)


def halo(near, far):
    count = lax.axis_size(XY)
    near = lax.ppermute(near, XY, [(i, i ^ 1) for i in range(count)])
    around = [((i + 1) % count, ((i ^ 1) + 1) % count) for i in range(count)]
    return near, lax.ppermute(far, XY, around)


def apply_m(first, r, ps, inflow, first_inflow, tabs, other):
    outs = (FIELD, PLANE, PLANE, EDGE, EDGE, (2, 8, 128))
    return call(make_apply(first), outs, "apply", 8, scratch=SCR)(
        r, ps, *inflow, *first_inflow, tabs, other
    )


def operate(u, kc, zlow, zup):
    return call(operator, (FIELD,), "operator", 4, scratch=(PLANE,))(u, kc, zlow, zup)[0]


def per_device(load, mat, lay, stf, cpl, piv, fac):
    hbm_args = [load, mat, lay] + [jnp.transpose(t, (1, 2, 0)) for t in (fac, piv, stf, cpl)]
    hbm_args = [pltpu.with_memory_space_constraint(v, pltpu.HBM) for v in hbm_args]
    keep, give, tabs, load, ps, kc = call(
        first_sweep,
        (part_of(37), part_of(37), TABS, FIELD, PS, KC),
        "first_sweep",
        7,
        hbm=range(7),
        scratch=[pltpu.VMEM(mat.shape, I32), pltpu.VMEM(lay.shape, I32), (6, 34, 8, 128)]
        + [pltpu.SMEM(v.shape, F32) for v in hbm_args[3:]],
        sems=((3, NZ), (4,)),
    )(*hbm_args)
    lu, *send = call(
        make_merge(True), ((2, *part_of(37)), *blocks_of(R1)), "merge1", 3, scratch=((NSEG * R1, 128),)
    )(keep, swap(give), tabs)
    fixed, *back = call(
        make_owner(True),
        ((NSEG * R1, 128), *blocks_of(R2)),
        "owner1",
        NSEG + 1,
        scratch=((NSEG * R2, 128),),
    )(*exchange(send), tabs)
    keep, give, back1 = call(
        make_split(True), (part_of(11), part_of(11), (NSEG * R2, 128)), "split1", NSEG + 2
    )(*exchange(back), lu, tabs)
    inflow1 = (keep, swap(give))
    u, zlow, zup, near, far, da = apply_m(True, load, ps, inflow1, inflow1, tabs, load)
    near, far = halo(near, far)
    part = operate(u, kc, zlow, zup)
    image, keep, give, dc = call(
        second_sweep, (FIELD, part_of(8), part_of(8), (1, 8, 128)), "second_sweep", 5, scratch=SCR
    )(part, near, far, u, ps)
    lu2, *send = call(
        make_merge(False), ((2, *part_of(8)), *blocks_of(R3)), "merge2", 4, scratch=((NSEG * R3, 128),)
    )(keep, swap(give), lu, tabs)
    back = call(
        make_owner(False), blocks_of(R3), "owner2", NSEG + 2, scratch=((NSEG * R3, 128),) * 2
    )(*exchange(send), fixed, tabs)
    keep, give = call(
        make_split(False), (part_of(8),) * 2, "split2", NSEG + 4, scratch=((NSEG * R3, 128),)
    )(*exchange(back), lu2, lu, back1, tabs)
    w, zlow, zup, near, far, db = apply_m(False, image, ps, (keep, swap(give)), inflow1, tabs, load)
    near, far = halo(near, far)
    part = operate(w, kc, zlow, zup)
    y, sums = call(last_dots, (FIELD, (128, 1, 128)), "last_dots", 8)(part, near, far, u, w, da, db, dc)
    sums = lax.all_to_all(sums, ALL, 0, 0, tiled=True)
    return tuple(call(combine, (FIELD, FIELD), "combine", 6)(sums, load, u, image, w, y))


def solution(mesh):
    finer = Mesh(mesh.devices.reshape(4, 2, 4, 4), ALL)
    return jax.shard_map(
        per_device,
        mesh=finer,
        in_specs=(P(GZ, None, XY, None), P(GZ, XY, None), P(GZ, XY, None), P(), P(), P(), P()),
        out_specs=(P(GZ, None, XY, None), P(GZ, None, XY, None)),
        check_vma=False,
    )
```

```python
import jax
import jax.numpy as jnp
from jax import lax
from jax.experimental import pallas as pl
from jax.experimental.pallas import tpu as pltpu
from jax.sharding import Mesh
from jax.sharding import PartitionSpec as P

GZ = ("gz_0", "gz_1")
XY = ("xy_0", "xy_1")
ALL = GZ + XY
F32 = jnp.float32
I32 = jnp.int32

NZ = 16
CHUNK = 4
NSEG = 4
COLS = [(xi, lj) for xi in range(2) for lj in range(3)]
SYM = [(i, j) for i in range(4) for j in range(i, 4)]
SYMI = {}
for _n, (_i, _j) in enumerate(SYM):
    SYMI[(_i, _j)] = _n
    SYMI[(_j, _i)] = _n
T_P, T_S, T_K, T_C, T_L = 0, 16, 26, 36, 46
NTAB = 56
NONE = 127
R1, R2, R3 = 224, 72, 56
MIB = 1 << 20


def tile(xi, lj):
    return pl.ds(8 * xi, 8), pl.ds(128 * lj, 128)


def look(tabs, first, count, ids):
    return [
        jnp.take_along_axis(tabs[first + e], ids, axis=1, mode="promise_in_bounds")
        for e in range(count)
    ]


def fsum(terms):
    terms = list(terms)
    while len(terms) > 1:
        terms = [
            terms[n] + terms[n + 1] if n + 1 < len(terms) else terms[n]
            for n in range(0, len(terms), 2)
        ]
    return terms[0]


def full(blk, v):
    return [fsum(blk[4 * i + j] * v[j] for j in range(4)) for i in range(4)]


def full_t(blk, v):
    return [fsum(blk[4 * i + j] * v[i] for i in range(4)) for j in range(4)]


def symm(blk, v):
    return [fsum(blk[SYMI[(i, j)]] * v[j] for j in range(4)) for i in range(4)]


def lower_t(low, v):
    return [fsum(low[SYMI[(i, j)]] * v[j] for j in range(i, 4)) for i in range(4)]


def add(a, b):
    return [x + y for x, y in zip(a, b)]


def half():
    return lax.axis_index("gz_1")


def xy_index():
    return lax.axis_size("xy_1") * lax.axis_index("xy_0") + lax.axis_index("xy_1")


def block(chip, per):
    return pl.ds(pl.multiple_of(chip * per, 8), per)


def to_partners(blocks, outs, per):
    me = lax.axis_index("gz_0")
    for d, out in enumerate(outs):
        out[...] = blocks[block(jnp.bitwise_xor(me, d), per), :]


def from_partners(parts, blocks, per):
    me = lax.axis_index("gz_0")
    for d, part in enumerate(parts):
        blocks[block(jnp.bitwise_xor(me, d), per), :] = part[...]


def put_rows(send, per, v, lj, value):
    send[pl.ds(6 * v + lj, 4, stride=per), :] = value[:4]
    send[pl.ds(6 * v + 3 + lj, 4, stride=per), :] = value[4:]


def get_rows(recv, per, v, lj):
    low = recv[pl.ds(6 * v + lj, 4, stride=per), :]
    high = recv[pl.ds(6 * v + 3 + lj, 4, stride=per), :]
    return jnp.concatenate([low, high], axis=0)


def build_tables(tabs, fac, piv, stf, cpl):
    lane = lax.broadcasted_iota(I32, (8, 128), 1)
    zero = jnp.zeros((8, 128), F32)
    for src, first, count, pairs in (
        (fac, T_P, 6, [(i, j) for i in range(4) for j in range(4)]),
        (piv, T_S, 8, SYM),
        (stf, T_K, 8, SYM),
        (cpl, T_C, 6, SYM),
    ):
        for e, (i, j) in enumerate(pairs):
            row = zero
            for m in range(count):
                row = jnp.where(lane == m, src[i, j, m], row)
            tabs[first + e] = row
    low = {}
    for j in range(4):
        diag = tabs[T_S + SYMI[(j, j)]]
        rest = diag
        for k in range(j):
            rest = rest - low[(j, k)] * low[(j, k)]
        good = rest > 1e-7 * diag
        safe = jnp.where(good, rest, 1.0)
        inv = lax.rsqrt(safe)
        inv = inv * (1.5 - 0.5 * safe * inv * inv)
        inv = jnp.where(good, inv, 0.0)
        low[(j, j)] = safe * inv
        for i in range(j + 1, 4):
            part = tabs[T_S + SYMI[(i, j)]]
            for k in range(j):
                part = part - low[(i, k)] * low[(j, k)]
            low[(i, j)] = part * inv
    for (i, j), value in low.items():
        tabs[T_L + SYMI[(i, j)]] = value


def first_sweep(
    r_hbm, mat_hbm, lay_hbm, *refs
):
    tables, (keep, give, tabs, r, mat, lay, pb), (st, fac, piv, stf, cpl, sems, table_sems) = (
        refs[:4],
        refs[4:11],
        refs[11:],
    )
    loads = [
        pltpu.make_async_copy(src, dst, table_sems.at[e])
        for e, (src, dst) in enumerate(zip(tables, (fac, piv, stf, cpl)))
    ]
    for cp in loads:
        cp.start()

    def copies(part):
        at = pl.ds(part * CHUNK, CHUNK)
        return [
            pltpu.make_async_copy(src.at[at], dst.at[at], sems.at[e, part])
            for e, (src, dst) in enumerate(((r_hbm, r), (mat_hbm, mat), (lay_hbm, lay)))
        ]

    for part in range(NZ // CHUNK):
        for cp in copies(part):
            cp.start()
    for cp in loads:
        cp.wait()
    build_tables(tabs, fac, piv, stf, cpl)
    for cp in copies(0):
        cp.wait()
    zero = jnp.zeros((8, 128), F32)
    one = jnp.ones((8, 128), F32)
    G, X, Q, W = 0, 4, 20, 30

    def blocks(z, n, rows, lanes):
        blk = look(tabs, T_P, 16, lay[z, rows, lanes])
        for e in range(16):
            pb[z, n, e] = blk[e]
        return blk, look(tabs, T_L, 10, mat[z, rows, lanes])

    for n, (xi, lj) in enumerate(COLS):
        rows, lanes = tile(xi, lj)
        g = [r[0, c, rows, lanes] for c in range(4)]
        _, low = blocks(0, n, rows, lanes)
        q = [
            fsum(low[SYMI[(i, k)]] * low[SYMI[(j, k)]] for k in range(min(i, j) + 1)) for i, j in SYM
        ]
        x = [one if i == c else zero for c in range(4) for i in range(4)]
        for v, value in enumerate(g + x + q + symm(q, g)):
            st[n, v] = value

    def level(z, carry):
        @pl.when(z % CHUNK == 0)
        def _():
            for cp in copies(z // CHUNK):
                cp.wait()

        for n, (xi, lj) in enumerate(COLS):
            rows, lanes = tile(xi, lj)
            blk, piv_blk = blocks(z, n, rows, lanes)
            g = full(blk, [st[n, G + c] for c in range(4)])
            g = add([r[z, c, rows, lanes] for c in range(4)], g)
            for c in range(4):
                st[n, G + c] = g[c]
            x = [full(blk, [st[n, X + 4 * c + i] for i in range(4)]) for c in range(4)]
            for c in range(4):
                for i in range(4):
                    st[n, X + 4 * c + i] = x[c][i]
            h = lower_t(piv_blk, g)
            x = [lower_t(piv_blk, x[c]) for c in range(4)]
            for c in range(4):
                st[n, W + c] += fsum(x[c][i] * h[i] for i in range(4))
            for c in range(4):
                for d in range(c + 1):
                    st[n, Q + SYMI[(d, c)]] += fsum(x[d][i] * x[c][i] for i in range(4))
        return carry

    lax.fori_loop(1, NZ, level, 0)
    for core in range(2):

        @pl.when(half() == core)
        def _():
            for n, (xi, lj) in enumerate(COLS):
                rows, lanes = tile(xi, lj)
                values = [st[n, v] for v in (*range(4), *range(W, W + 4))]
                values += [st[n, X + 4 * j + i] for i in range(4) for j in range(4)]
                values += [st[n, Q + e] for e in range(10)]
                ids = [lay[0, rows, lanes], lay[NZ - 1, rows, lanes], mat[NZ - 1, rows, lanes]]
                for v, value in enumerate(values + [d.astype(F32) for d in ids]):
                    (keep if xi == core else give)[v, lj] = value


def expand(mat, lay, tabs, after, sb, kc, token):
    token[...] = after[:8]

    def level(z, carry):
        for n, (xi, lj) in enumerate(COLS):
            rows, lanes = tile(xi, lj)
            lay_ids, mat_ids = lay[z, rows, lanes], mat[z, rows, lanes]
            for e, value in enumerate(look(tabs, T_S, 10, mat_ids)):
                sb[z, n, e] = value
            for e, value in enumerate(look(tabs, T_K, 10, mat_ids) + look(tabs, T_C, 10, lay_ids)):
                kc[z, n, e] = value
        return carry

    lax.fori_loop(0, NZ, level, 0)


def make_merge(first):
    count, per = (37, R1) if first else (8, R3)

    def merge(*refs):
        send = refs[-1]
        if first:
            keep, got, tabs, lu, *outs = refs[:-1]
            fixed = lu
        else:
            keep, got, fixed, tabs, lu, *outs = refs[:-1]
        lower = half() == 0
        for lj in range(3):
            for v in range(count):
                mine, other = keep[v, lj], got[v, lj]
                lu[0, v, lj] = jnp.where(lower, mine, other)
                lu[1, v, lj] = jnp.where(lower, other, mine)
            bottom = look(tabs, T_P, 16, fixed[1, 34, lj].astype(I32))
            xl = [fixed[0, 8 + e, lj] for e in range(16)]
            xu = [fixed[1, 8 + e, lj] for e in range(16)]
            qu = [fixed[1, 24 + e, lj] for e in range(10)]
            y = [full(bottom, [xl[4 * i + c] for i in range(4)]) for c in range(4)]
            a = full(bottom, [lu[0, c, lj] for c in range(4)])
            o = add([lu[1, c, lj] for c in range(4)], full(xu, a))
            b = add([lu[1, 4 + c, lj] for c in range(4)], symm(qu, a))
            w = [lu[0, 4 + c, lj] + fsum(y[c][i] * b[i] for i in range(4)) for c in range(4)]
            values = o + w
            if first:
                xc = [full(xu, y[c]) for c in range(4)]
                values += [xc[j][i] for i in range(4) for j in range(4)]
                qy = [symm(qu, y[c]) for c in range(4)]
                values += [
                    fixed[0, 24 + e, lj] + fsum(y[d][i] * qy[c][i] for i in range(4))
                    for e, (d, c) in enumerate(SYM)
                ]
                values += [fixed[0, 34, lj], fixed[1, 35, lj], fixed[1, 36, lj]]
            for v, value in enumerate(values):
                put_rows(send, per, v, lj, value)
        to_partners(send, outs, per)

    return merge


def make_split(first):
    count, per = (11, R2) if first else (8, R3)

    def split(*refs):
        parts = refs[:NSEG]
        if first:
            lu, tabs, keep, give, back = refs[NSEG:]
            fixed, first_back = lu, back
        else:
            lu, fixed, first_back, tabs, keep, give, back = refs[NSEG:]
        from_partners(parts, back, per)
        lower = half() == 0
        for lj in range(3):
            g0 = [get_rows(back, per, c, lj) for c in range(4)]
            b1 = [get_rows(back, per, 4 + c, lj) for c in range(4)]
            ids = [get_rows(first_back, R2, 8 + e, lj) for e in range(3)]
            a0 = full(look(tabs, T_P, 16, fixed[0, 34, lj].astype(I32)), g0)
            g1 = full([fixed[0, 8 + e, lj] for e in range(16)], a0)
            g1 = add([lu[0, c, lj] for c in range(4)], g1)
            a1 = full(look(tabs, T_P, 16, fixed[1, 34, lj].astype(I32)), g1)
            t = full_t(look(tabs, T_P, 16, ids[0].astype(I32)), b1)
            b0 = add(
                symm([fixed[1, 24 + e, lj] for e in range(10)], a1),
                full_t([fixed[1, 8 + e, lj] for e in range(16)], t),
            )
            b0 = add([lu[1, 4 + c, lj] for c in range(4)], b0)
            low = g0 + b0 + [fixed[1, 34, lj], ids[1], ids[2]]
            high = g1 + b1 + [ids[0], fixed[0, 35, lj], fixed[0, 36, lj]]
            for v in range(count):
                keep[v, lj] = jnp.where(lower, low[v], high[v])
                give[v, lj] = jnp.where(lower, high[v], low[v])

    return split


def make_owner(first):
    out_rows = R2 if first else R3

    def owner(*refs):
        parts, back = refs[:NSEG], refs[-1]
        if first:
            tabs, _, recv, *outs = refs[NSEG:-1]
            fixed = recv
        else:
            fixed, tabs, *outs = refs[NSEG:-2]
            recv = refs[-2]
        from_partners(parts, recv, R1 if first else R3)

        def get(ref, per, k, v):
            return ref[pl.ds(per * k + 6 * v, 8), :]

        per = R1 if first else R3

        def ident(k, v):
            return jnp.bitwise_and(get(fixed, R1, k, v).astype(I32), 127)

        zero = jnp.zeros((8, 128), F32)
        state = [zero] * 4
        inflow = []
        bottoms = []
        for k in range(NSEG):
            for c in range(4):
                back[pl.ds(out_rows * k + 6 * c, 6), :] = state[c][:6]
            bottom = look(tabs, T_P, 16, ident(k, 34))
            bottoms.append(bottom)
            a = full(bottom, state)
            inflow.append(a)
            if k < NSEG - 1:
                x = [get(fixed, R1, k, 8 + e) for e in range(16)]
                state = add([get(recv, per, k, c) for c in range(4)], full(x, a))
        b = [zero] * 4
        t = [zero] * 4
        for k in reversed(range(NSEG)):
            for c in range(4):
                back[pl.ds(out_rows * k + 24 + 6 * c, 6), :] = b[c][:6]
            if k > 0:
                q = [get(fixed, R1, k, 24 + e) for e in range(10)]
                wb = add([get(recv, per, k, 4 + c) for c in range(4)], symm(q, inflow[k]))
                if k < NSEG - 1:
                    x = [get(fixed, R1, k, 8 + e) for e in range(16)]
                    wb = add(wb, full_t(x, t))
                b = wb
                t = full_t(bottoms[k], b)
        if first:
            none = jnp.full((6, 128), float(NONE), F32)
            for k in range(NSEG):
                above = get(fixed, R1, k + 1, 34)[:6] if k + 1 < NSEG else none
                back[pl.ds(R2 * k + 48, 6), :] = above
                for e in range(2):
                    below = get(fixed, R1, k - 1, 35 + e)[:6] if k > 0 else none
                    back[pl.ds(R2 * k + 54 + 6 * e, 6), :] = below
                back[pl.ds(R2 * k + 66, 6), :] = none
        to_partners(back, outs, out_rows)

    return owner


def make_apply(first):
    def apply(r, pb, sb, keep, got, first_keep, first_got, tabs, other, u, zlow, zup, near, far, dots, hscr, st):
        core = half()

        def get(n, v, own=keep, other=got):
            xi, lj = COLS[n]
            return jnp.where(core == xi, own[v, lj], other[v, lj])

        for n in range(6):
            for c in range(4):
                st[n, c] = get(n, c)

        def up(z, carry):
            for n, (xi, lj) in enumerate(COLS):
                rows, lanes = tile(xi, lj)
                g = full([pb[z, n, e] for e in range(16)], [st[n, c] for c in range(4)])
                g = add([r[z, c, rows, lanes] for c in range(4)], g)
                for c in range(4):
                    st[n, c] = g[c]
                h = symm([sb[z, n, e] for e in range(10)], g)
                for c in range(4):
                    hscr[z, n, c] = h[c]
            return carry

        lax.fori_loop(0, NZ, up, 0)
        zero = jnp.zeros((8, 128), F32)
        for n, (xi, lj) in enumerate(COLS):
            rows, lanes = tile(xi, lj)
            b = [get(n, 4 + c) for c in range(4)]
            t = full_t(look(tabs, T_P, 16, get(n, 8, first_keep, first_got).astype(I32)), b)
            for c in range(4):
                zup[c, rows, lanes] = b[c]
                st[n, c] = t[c]

        def down(s, carry):
            z = NZ - 1 - s
            ar, ao = carry
            for n, (xi, lj) in enumerate(COLS):
                rows, lanes = tile(xi, lj)
                w = [hscr[z, n, c] + st[n, c] for c in range(4)]
                for c in range(4):
                    u[z, c, rows, lanes] = w[c]
                ar = ar + fsum(w[c] * r[z, c, rows, lanes] for c in range(4))
                if not first:
                    ao = ao + fsum(w[c] * other[z, c, rows, lanes] for c in range(4))
                t = full_t([pb[z, n, e] for e in range(16)], w)
                for c in range(4):
                    st[n, c] = t[c]
            return ar, ao

        acc_r, acc_o = lax.fori_loop(0, NZ, down, (zero, zero))
        dots[0] = acc_r
        dots[1] = acc_o
        for n, (xi, lj) in enumerate(COLS):
            rows, lanes = tile(xi, lj)
            lay_id, mat_id = [get(n, 9 + e, first_keep, first_got).astype(I32) for e in range(2)]
            below = symm(look(tabs, T_S, 10, mat_id), [get(n, c) for c in range(4)])
            below = add(below, [st[n, c] for c in range(4)])
            pushed = symm(look(tabs, T_C, 10, lay_id), below)
            for c in range(4):
                zlow[c, rows, lanes] = pushed[c]

        even = xy_index() % 2 == 0

        def edges(z, carry):
            for c in range(4):
                first_row, last_row = u[z, c, pl.ds(0, 1), :], u[z, c, pl.ds(15, 1), :]
                near[z, pl.ds(c, 1), :] = jnp.where(even, last_row, first_row)
                far[z, pl.ds(c, 1), :] = jnp.where(even, first_row, last_row)
            return carry

        lax.fori_loop(0, NZ, edges, 0)

    return apply


def operator(u, kc, zlow, zup, out, dots, push):
    col = lax.broadcasted_iota(I32, (8, 384), 1)
    row = lax.broadcasted_iota(I32, (8, 384), 0)
    push[...] = zlow[...]

    def level(z, acc):
        for xi in range(2):
            rows = pl.ds(8 * xi, 8)
            side = []
            for c in range(4):
                here = u[z, c, rows, :]
                west = jnp.where(col == 0, 0.0, pltpu.roll(here, 1, 1))
                east = jnp.where(col == 383, 0.0, pltpu.roll(here, 383, 1))
                other = u[z, c, pl.ds(8 * (1 - xi), 8), :]
                down = pltpu.roll(here, 1, 0)
                upw = pltpu.roll(here, 7, 0)
                if xi == 0:
                    down = jnp.where(row == 0, 0.0, down)
                    upw = jnp.where(row == 7, pltpu.roll(other, 7, 0), upw)
                else:
                    down = jnp.where(row == 0, pltpu.roll(other, 1, 0), down)
                    upw = jnp.where(row == 7, 0.0, upw)
                side.append((west + east) + (down + upw))
            for lj in range(3):
                lanes = pl.ds(128 * lj, 128)
                v = [u[z, c, rows, lanes] for c in range(4)]
                nz = jnp.minimum(z + 1, NZ - 1)
                above = [
                    jnp.where(z == NZ - 1, zup[c, rows, lanes], u[nz, c, rows, lanes])
                    for c in range(4)
                ]
                n = 3 * xi + lj
                kv = symm([kc[z, n, e] for e in range(10)], v)
                cb = [kc[z, n, 10 + e] for e in range(10)]
                fa = symm(cb, above)
                fb = symm(cb, v)
                val = []
                for c in range(4):
                    near = side[c][:, 128 * lj : 128 * (lj + 1)]
                    val.append(kv[c] - near - fa[c] - push[c, rows, lanes])
                    out[z, c, rows, lanes] = val[c]
                    push[c, rows, lanes] = fb[c]
                acc = acc + fsum(val[c] * v[c] for c in range(4))
        return acc

    dots[0] = lax.fori_loop(0, NZ, level, jnp.zeros((8, 128), F32))


def edge_dot(near, far, own_near, own_far):
    index = xy_index()
    last = lax.axis_size("xy_0") * lax.axis_size("xy_1") - 1
    inside = (index > 0) & (index < last)
    outer = jnp.where(inside, far[...], 0.0) * own_far[...]
    return jnp.sum(near[...] * own_near[...] + outer, axis=0)


def halo_masks():
    row = lax.broadcasted_iota(I32, (8, 128), 0)
    index = xy_index()
    last = lax.axis_size("xy_0") * lax.axis_size("xy_1") - 1
    return index % 2 == 0, ((row == 0) & (index > 0), (row == 7) & (index < last))


def with_halo(part, near, far, z, c, xi, lj, masks):
    rows, lanes = tile(xi, lj)
    even, inside = masks
    a, b = near[z, pl.ds(c, 1), lanes], far[z, pl.ds(c, 1), lanes]
    edge = jnp.where(even, b, a) if xi == 0 else jnp.where(even, a, b)
    return part[z, c, rows, lanes] - jnp.where(inside[xi], edge, 0.0)


def second_sweep(part, near, far, pb, sb, image, keep, give, hscr, st):
    masks = halo_masks()
    zero = jnp.zeros((8, 128), F32)
    for n in range(6):
        for c in range(4):
            st[n, c] = zero

    def up(z, carry):
        for n, (xi, lj) in enumerate(COLS):
            rows, lanes = tile(xi, lj)
            blk = [pb[z, n, e] for e in range(16)]
            img = [with_halo(part, near, far, z, c, xi, lj, masks) for c in range(4)]
            for c in range(4):
                image[z, c, rows, lanes] = img[c]
            g = add(img, full(blk, [st[n, c] for c in range(4)]))
            for c in range(4):
                st[n, c] = g[c]
            h = symm([sb[z, n, e] for e in range(10)], g)
            for c in range(4):
                hscr[z, n, c] = h[c]
        return carry

    lax.fori_loop(0, NZ, up, 0)
    up_last = []
    for n in range(6):
        for c in range(4):
            up_last.append(st[n, c])
            st[n, c] = hscr[NZ - 1, n, c]

    def down(s, carry):
        z = NZ - 2 - s
        for n in range(6):
            t = full_t([pb[z + 1, n, e] for e in range(16)], [st[n, c] for c in range(4)])
            for c in range(4):
                st[n, c] = hscr[z, n, c] + t[c]
        return carry

    for core in range(2):

        @pl.when(half() == core)
        def _():
            for n, (xi, lj) in enumerate(COLS):
                for c in range(4):
                    (keep if xi == core else give)[c, lj] = up_last[4 * n + c]

    lax.fori_loop(0, NZ - 1, down, 0)
    for core in range(2):

        @pl.when(half() == core)
        def _():
            for n, (xi, lj) in enumerate(COLS):
                for c in range(4):
                    (keep if xi == core else give)[4 + c, lj] = st[n, c]


def last_dots(near, far, *refs):
    (near_w, far_w, nu, fu, own_nu, own_fu), (da, db, dc, dd, sums) = refs[:6], refs[6:]
    lane = lax.broadcasted_iota(I32, (1, 128), 1)
    line = jnp.zeros((1, 128), F32)
    curv0 = jnp.sum(dc[0]) - jnp.sum(edge_dot(nu, fu, own_nu, own_fu))
    curv1 = jnp.sum(dd[0]) - jnp.sum(edge_dot(near, far, near_w, far_w))
    for e, value in enumerate((jnp.sum(da[0]), curv0, jnp.sum(db[0]), jnp.sum(db[1]), curv1)):
        line = jnp.where(lane == e, value, line)
    sums[...] = jnp.broadcast_to(line[None], sums.shape)


def combine(sums, r, u, image, w, part, near, far, sol_hbm, res_hbm, sol, res, sems):
    tot = fsum([jnp.sum(sums[pl.ds(16 * k, 16)], axis=0) for k in range(8)])
    ru, ui, iw, rw, wy = [tot[:, e : e + 1] for e in range(5)]
    a0 = ru / ui
    fresh = ru - a0 * (rw + ui) + a0 * a0 * iw
    beta1 = 1.0 + fresh / ru
    curv = beta1 * beta1 * ui - beta1 * a0 * (iw + iw) + a0 * a0 * wy
    a1 = fresh / curv
    s0 = jnp.broadcast_to(a0 + a1 * beta1, (8, 128))
    s1 = jnp.broadcast_to(a1 * a0, (8, 128))
    masks = halo_masks()

    def copies(z):
        return [
            pltpu.make_async_copy(src.at[z], dst.at[z], sems.at[e, z])
            for e, (src, dst) in enumerate(((sol, sol_hbm), (res, res_hbm)))
        ]

    def level(z, carry):
        for xi, lj in COLS:
            rows, lanes = tile(xi, lj)
            for c in range(4):
                at = (z, c, rows, lanes)
                sol[at] = s0 * u[at] - s1 * w[at]
                y = with_halo(part, near, far, z, c, xi, lj, masks)
                res[at] = r[at] - s0 * image[at] + s1 * y
        for cp in copies(z):
            cp.start()
        return carry

    lax.fori_loop(0, NZ, level, 0)

    def finish(z, carry):
        for cp in copies(z):
            cp.wait()
        return carry

    lax.fori_loop(0, NZ, finish, 0)


def call(body, out, name, nargs, hbm=(), scratch=(), sems=(), limit=10, to_hbm=False):
    vm = pl.BlockSpec(memory_space=pltpu.VMEM)
    hb = pl.BlockSpec(memory_space=pltpu.HBM)
    return pl.pallas_call(
        body,
        out_shape=[s if hasattr(s, "dtype") else jax.ShapeDtypeStruct(s, F32) for s in out],
        in_specs=[hb if n in hbm else vm for n in range(nargs)],
        out_specs=[hb if to_hbm else vm for _ in out],
        scratch_shapes=[s if hasattr(s, "dtype") else pltpu.VMEM(s, F32) for s in scratch]
        + [pltpu.SemaphoreType.DMA(s) for s in sems],
        compiler_params=pltpu.CompilerParams(vmem_limit_bytes=limit * MIB),
        name=name,
    )


FIELD = (NZ, 4, 16, 384)
EDGE = (NZ, 4, 384)
PLANE = (4, 16, 384)
TABS = (NTAB, 8, 128)
SCR = ((NZ, 6, 4, 8, 128), (6, 4, 8, 128))
PB = (NZ, 6, 16, 8, 128)
SB = (NZ, 6, 10, 8, 128)
KC = (NZ, 6, 20, 8, 128)


def exchange(parts):
    count = lax.axis_size("gz_0")
    moved = [
        lax.ppermute(part, "gz_0", [(i, i ^ d) for i in range(count)])
        for d, part in enumerate(parts)
        if d > 0
    ]
    return [parts[0]] + moved


def blocks_of(per):
    return [(per, 128)] * NSEG


def swap(buf):
    return lax.ppermute(buf, "gz_1", [(0, 1), (1, 0)])


def part_of(count):
    return (count, 3, 8, 128)


def halo(near, far):
    count = lax.axis_size(XY)
    near = lax.ppermute(near, XY, [(i, i ^ 1) for i in range(count)])
    around = [((i + 1) % count, ((i ^ 1) + 1) % count) for i in range(count)]
    return near, lax.ppermute(far, XY, around)


def apply_m(first, r, pb, sb, inflow, first_inflow, tabs, other):
    outs = (FIELD, PLANE, PLANE, EDGE, EDGE, (2, 8, 128))
    return call(make_apply(first), outs, "apply", 9, scratch=SCR)(
        r, pb, sb, *inflow, *first_inflow, tabs, other
    )


def operate(u, kc, zlow, zup):
    return call(operator, (FIELD, (1, 8, 128)), "operator", 4, scratch=(PLANE,))(u, kc, zlow, zup)


def per_device(load, mat, lay, stf, cpl, piv, fac):
    hbm_args = [load, mat, lay] + [jnp.transpose(t, (1, 2, 0)) for t in (fac, piv, stf, cpl)]
    hbm_args = [pltpu.with_memory_space_constraint(v, pltpu.HBM) for v in hbm_args]
    ids = [jax.ShapeDtypeStruct(v.shape, I32) for v in (mat, lay)]
    keep, give, tabs, load, mat, lay, pb = call(
        first_sweep,
        (part_of(37), part_of(37), TABS, FIELD, *ids, PB),
        "first_sweep",
        7,
        hbm=range(7),
        scratch=[(6, 34, 8, 128)] + [pltpu.SMEM(v.shape, F32) for v in hbm_args[3:]],
        sems=((3, NZ // CHUNK), (4,)),
    )(*hbm_args)
    lu, *send = call(
        make_merge(True), ((2, *part_of(37)), *blocks_of(R1)), "merge1", 3, scratch=((NSEG * R1, 128),)
    )(keep, swap(give), tabs)
    sent = exchange(send)
    sb, kc, token = call(expand, (SB, KC, (8, 128)), "expand", 4)(mat, lay, tabs, send[0])
    fixed, *back = call(
        make_owner(True),
        ((NSEG * R1, 128), *blocks_of(R2)),
        "owner1",
        NSEG + 2,
        scratch=((NSEG * R2, 128),),
    )(*sent, tabs, token)
    keep, give, back1 = call(
        make_split(True), (part_of(11), part_of(11), (NSEG * R2, 128)), "split1", NSEG + 2
    )(*exchange(back), lu, tabs)
    inflow1 = (keep, swap(give))
    u, zlow, zup, near_u, far_u, da = apply_m(True, load, pb, sb, inflow1, inflow1, tabs, load)
    edges_u = halo(near_u, far_u)
    part, dc = operate(u, kc, zlow, zup)
    image, keep, give = call(
        second_sweep, (FIELD, part_of(8), part_of(8)), "second_sweep", 5, scratch=SCR
    )(part, *edges_u, pb, sb)
    lu2, *send = call(
        make_merge(False), ((2, *part_of(8)), *blocks_of(R3)), "merge2", 4, scratch=((NSEG * R3, 128),)
    )(keep, swap(give), lu, tabs)
    back = call(
        make_owner(False), blocks_of(R3), "owner2", NSEG + 2, scratch=((NSEG * R3, 128),) * 2
    )(*exchange(send), fixed, tabs)
    keep, give = call(
        make_split(False), (part_of(8),) * 2, "split2", NSEG + 4, scratch=((NSEG * R3, 128),)
    )(*exchange(back), lu2, lu, back1, tabs)
    w, zlow, zup, near_w, far_w, db = apply_m(
        False, image, pb, sb, (keep, swap(give)), inflow1, tabs, load
    )
    edges_w = halo(near_w, far_w)
    part, dd = operate(w, kc, zlow, zup)
    (sums,) = call(last_dots, ((128, 1, 128),), "last_dots", 12)(
        *edges_w, near_w, far_w, *edges_u, near_u, far_u, da, db, dc, dd
    )
    sums = lax.all_to_all(sums, ALL, 0, 0, tiled=True)
    return tuple(
        call(
            combine,
            (FIELD, FIELD),
            "combine",
            8,
            scratch=(FIELD, FIELD),
            sems=((2, NZ),),
            to_hbm=True,
        )(sums, load, u, image, w, part, *edges_w)
    )


def solution(mesh):
    finer = Mesh(mesh.devices.reshape(4, 2, 4, 4), ALL)
    return jax.shard_map(
        per_device,
        mesh=finer,
        in_specs=(P(GZ, None, XY, None), P(GZ, XY, None), P(GZ, XY, None), P(), P(), P(), P()),
        out_specs=(P(GZ, None, XY, None), P(GZ, None, XY, None)),
        check_vma=False,
    )
```

```python
import jax
import jax.numpy as jnp
from jax import lax
from jax.experimental import pallas as pl
from jax.experimental.pallas import tpu as pltpu
from jax.sharding import Mesh
from jax.sharding import PartitionSpec as P


GZ = ("gz_0", "gz_1")
XY = ("xy_0", "xy_1")
ALL = GZ + XY
F32 = jnp.float32
I32 = jnp.int32

NZ = 16
CHUNK = 4
NSEG = 4
COLS = [(xi, lj) for xi in range(2) for lj in range(3)]
SYM = [(i, j) for i in range(4) for j in range(i, 4)]
SYMI = {}
for _n, (_i, _j) in enumerate(SYM):
    SYMI[(_i, _j)] = _n
    SYMI[(_j, _i)] = _n
T_P, T_S, T_K, T_C, T_L = 0, 16, 26, 36, 46
NTAB = 56
NONE = 127
R1, R2 = 224, 72
MIB = 1 << 20


def tile(xi, lj):
    return pl.ds(8 * xi, 8), pl.ds(128 * lj, 128)


def look(tabs, first, count, ids):
    return [
        jnp.take_along_axis(tabs[first + e], ids, axis=1, mode="promise_in_bounds")
        for e in range(count)
    ]


def fsum(terms):
    terms = list(terms)
    while len(terms) > 1:
        terms = [
            terms[n] + terms[n + 1] if n + 1 < len(terms) else terms[n]
            for n in range(0, len(terms), 2)
        ]
    return terms[0]


def full(blk, v):
    return [fsum(blk[4 * i + j] * v[j] for j in range(4)) for i in range(4)]


def full_t(blk, v):
    return [fsum(blk[4 * i + j] * v[i] for i in range(4)) for j in range(4)]


def symm(blk, v):
    return [fsum(blk[SYMI[(i, j)]] * v[j] for j in range(4)) for i in range(4)]


def lower_t(low, v):
    return [fsum(low[SYMI[(i, j)]] * v[j] for j in range(i, 4)) for i in range(4)]


def add(a, b):
    return [x + y for x, y in zip(a, b)]


def half():
    return lax.axis_index("gz_1")


def xy_index():
    return lax.axis_size("xy_1") * lax.axis_index("xy_0") + lax.axis_index("xy_1")


def block(chip, per):
    return pl.ds(pl.multiple_of(chip * per, 8), per)


def to_partners(blocks, outs, per):
    me = lax.axis_index("gz_0")
    for d, out in enumerate(outs):
        out[...] = blocks[block(jnp.bitwise_xor(me, d), per), :]


def from_partners(parts, blocks, per):
    me = lax.axis_index("gz_0")
    for d, part in enumerate(parts):
        blocks[block(jnp.bitwise_xor(me, d), per), :] = part[...]


def put_rows(send, per, v, lj, value):
    send[pl.ds(6 * v + lj, 4, stride=per), :] = value[:4]
    send[pl.ds(6 * v + 3 + lj, 4, stride=per), :] = value[4:]


def get_rows(recv, per, v, lj):
    low = recv[pl.ds(6 * v + lj, 4, stride=per), :]
    high = recv[pl.ds(6 * v + 3 + lj, 4, stride=per), :]
    return jnp.concatenate([low, high], axis=0)


def build_tables(tabs, fac, piv, stf, cpl):
    lane = lax.broadcasted_iota(I32, (8, 128), 1)
    zero = jnp.zeros((8, 128), F32)
    for src, first, count, pairs in (
        (fac, T_P, 6, [(i, j) for i in range(4) for j in range(4)]),
        (piv, T_S, 8, SYM),
        (stf, T_K, 8, SYM),
        (cpl, T_C, 6, SYM),
    ):
        for e, (i, j) in enumerate(pairs):
            row = zero
            for m in range(count):
                row = jnp.where(lane == m, src[i, j, m], row)
            tabs[first + e] = row
    low = {}
    for j in range(4):
        diag = tabs[T_S + SYMI[(j, j)]]
        rest = diag
        for k in range(j):
            rest = rest - low[(j, k)] * low[(j, k)]
        good = rest > 1e-7 * diag
        safe = jnp.where(good, rest, 1.0)
        inv = lax.rsqrt(safe)
        inv = inv * (1.5 - 0.5 * safe * inv * inv)
        inv = jnp.where(good, inv, 0.0)
        low[(j, j)] = safe * inv
        for i in range(j + 1, 4):
            part = tabs[T_S + SYMI[(i, j)]]
            for k in range(j):
                part = part - low[(i, k)] * low[(j, k)]
            low[(i, j)] = part * inv
    for (i, j), value in low.items():
        tabs[T_L + SYMI[(i, j)]] = value


def first_sweep(
    r_hbm, mat_hbm, lay_hbm, *refs
):
    tables, (keep, give, tabs, r, mat, lay, pb), (st, fac, piv, stf, cpl, sems, table_sems) = (
        refs[:4],
        refs[4:11],
        refs[11:],
    )
    loads = [
        pltpu.make_async_copy(src, dst, table_sems.at[e])
        for e, (src, dst) in enumerate(zip(tables, (fac, piv, stf, cpl)))
    ]
    for cp in loads:
        cp.start()

    def copies(part):
        at = pl.ds(part * CHUNK, CHUNK)
        return [
            pltpu.make_async_copy(src.at[at], dst.at[at], sems.at[e, part])
            for e, (src, dst) in enumerate(((r_hbm, r), (mat_hbm, mat), (lay_hbm, lay)))
        ]

    for part in range(NZ // CHUNK):
        for cp in copies(part):
            cp.start()
    for cp in loads:
        cp.wait()
    build_tables(tabs, fac, piv, stf, cpl)
    for cp in copies(0):
        cp.wait()
    zero = jnp.zeros((8, 128), F32)
    one = jnp.ones((8, 128), F32)
    G, X, Q, W = 0, 4, 20, 30

    def blocks(z, n, rows, lanes):
        blk = look(tabs, T_P, 16, lay[z, rows, lanes])
        for e in range(16):
            pb[z, n, e] = blk[e]
        return blk, look(tabs, T_L, 10, mat[z, rows, lanes])

    for n, (xi, lj) in enumerate(COLS):
        rows, lanes = tile(xi, lj)
        g = [r[0, c, rows, lanes] for c in range(4)]
        _, low = blocks(0, n, rows, lanes)
        q = [
            fsum(low[SYMI[(i, k)]] * low[SYMI[(j, k)]] for k in range(min(i, j) + 1)) for i, j in SYM
        ]
        x = [one if i == c else zero for c in range(4) for i in range(4)]
        for v, value in enumerate(g + x + q + symm(q, g)):
            st[n, v] = value

    def level(z, carry):
        @pl.when(z % CHUNK == 0)
        def _():
            for cp in copies(z // CHUNK):
                cp.wait()

        for n, (xi, lj) in enumerate(COLS):
            rows, lanes = tile(xi, lj)
            blk, piv_blk = blocks(z, n, rows, lanes)
            g = full(blk, [st[n, G + c] for c in range(4)])
            g = add([r[z, c, rows, lanes] for c in range(4)], g)
            for c in range(4):
                st[n, G + c] = g[c]
            x = [full(blk, [st[n, X + 4 * c + i] for i in range(4)]) for c in range(4)]
            for c in range(4):
                for i in range(4):
                    st[n, X + 4 * c + i] = x[c][i]
            h = lower_t(piv_blk, g)
            x = [lower_t(piv_blk, x[c]) for c in range(4)]
            for c in range(4):
                st[n, W + c] += fsum(x[c][i] * h[i] for i in range(4))
            for c in range(4):
                for d in range(c + 1):
                    st[n, Q + SYMI[(d, c)]] += fsum(x[d][i] * x[c][i] for i in range(4))
        return carry

    lax.fori_loop(1, NZ, level, 0)
    for core in range(2):

        @pl.when(half() == core)
        def _():
            for n, (xi, lj) in enumerate(COLS):
                rows, lanes = tile(xi, lj)
                values = [st[n, v] for v in (*range(4), *range(W, W + 4))]
                values += [st[n, X + 4 * j + i] for i in range(4) for j in range(4)]
                values += [st[n, Q + e] for e in range(10)]
                ids = [lay[0, rows, lanes], lay[NZ - 1, rows, lanes], mat[NZ - 1, rows, lanes]]
                for v, value in enumerate(values + [d.astype(F32) for d in ids]):
                    (keep if xi == core else give)[v, lj] = value


def expand(mat, lay, tabs, after, sb, kc, token):
    token[...] = after[:8]

    def level(z, carry):
        for n, (xi, lj) in enumerate(COLS):
            rows, lanes = tile(xi, lj)
            lay_ids, mat_ids = lay[z, rows, lanes], mat[z, rows, lanes]
            for e, value in enumerate(look(tabs, T_S, 10, mat_ids)):
                sb[z, n, e] = value
            for e, value in enumerate(look(tabs, T_K, 10, mat_ids) + look(tabs, T_C, 10, lay_ids)):
                kc[z, n, e] = value
        return carry

    lax.fori_loop(0, NZ, level, 0)


def make_merge(first):
    count = 37 if first else 8

    def merge(*refs):
        if first:
            keep, got, tabs, lu, maps, *outs, send = refs
            fixed = lu
        else:
            keep, got, fixed, tabs, lu, chip = refs
        lower = half() == 0
        for lj in range(3):
            for v in range(count):
                mine, other = keep[v, lj], got[v, lj]
                lu[0, v, lj] = jnp.where(lower, mine, other)
                lu[1, v, lj] = jnp.where(lower, other, mine)
            bottom = look(tabs, T_P, 16, fixed[1, 34, lj].astype(I32))
            xl = [fixed[0, 8 + e, lj] for e in range(16)]
            xu = [fixed[1, 8 + e, lj] for e in range(16)]
            qu = [fixed[1, 24 + e, lj] for e in range(10)]
            y = [full(bottom, [xl[4 * i + c] for i in range(4)]) for c in range(4)]
            a = full(bottom, [lu[0, c, lj] for c in range(4)])
            o = add([lu[1, c, lj] for c in range(4)], full(xu, a))
            b = add([lu[1, 4 + c, lj] for c in range(4)], symm(qu, a))
            w = [lu[0, 4 + c, lj] + fsum(y[c][i] * b[i] for i in range(4)) for c in range(4)]
            values = o + w
            if first:
                xc = [full(xu, y[c]) for c in range(4)]
                values += [xc[j][i] for i in range(4) for j in range(4)]
                qy = [symm(qu, y[c]) for c in range(4)]
                values += [
                    fixed[0, 24 + e, lj] + fsum(y[d][i] * qy[c][i] for i in range(4))
                    for e, (d, c) in enumerate(SYM)
                ]
                values += [fixed[0, 34, lj], fixed[1, 35, lj], fixed[1, 36, lj]]
            for v, value in enumerate(values):
                if first:
                    put_rows(send, R1, v, lj, value)
                else:
                    chip[v, lj] = value
            if first:
                for v in range(27):
                    maps[v, lj] = values[8 + v]
        if first:
            to_partners(send, outs, R1)

    return merge


def split_values(lu, fixed, tabs, lj, g0, b1, t):
    a0 = full(look(tabs, T_P, 16, fixed[0, 34, lj].astype(I32)), g0)
    g1 = full([fixed[0, 8 + e, lj] for e in range(16)], a0)
    g1 = add([lu[0, c, lj] for c in range(4)], g1)
    a1 = full(look(tabs, T_P, 16, fixed[1, 34, lj].astype(I32)), g1)
    b0 = add(
        symm([fixed[1, 24 + e, lj] for e in range(10)], a1),
        full_t([fixed[1, 8 + e, lj] for e in range(16)], t),
    )
    return g0 + add([lu[1, 4 + c, lj] for c in range(4)], b0), g1 + b1


def split(*refs):
    parts, (lu, tabs, keep, give, back) = refs[:NSEG], refs[NSEG:]
    from_partners(parts, back, R2)
    low_half = half() == 0
    for lj in range(3):
        g0 = [get_rows(back, R2, c, lj) for c in range(4)]
        b1 = [get_rows(back, R2, 4 + c, lj) for c in range(4)]
        ids = [get_rows(back, R2, 8 + e, lj) for e in range(3)]
        t = full_t(look(tabs, T_P, 16, ids[0].astype(I32)), b1)
        low, high = split_values(lu, lu, tabs, lj, g0, b1, t)
        low += [lu[1, 34, lj], ids[1], ids[2]]
        high += [ids[0], lu[0, 35, lj], lu[0, 36, lj]]
        for v in range(11):
            keep[v, lj] = jnp.where(low_half, low[v], high[v])
            give[v, lj] = jnp.where(low_half, high[v], low[v])


def scan(look_bottom, top, bottom, x, q):
    zero = jnp.zeros((8, 128), F32)
    below, inflow, factors = [[zero] * 4], [], []
    for k in range(NSEG):
        factors.append(look_bottom(k))
        inflow.append(full(factors[k], below[k]))
        if k < NSEG - 1:
            below.append(add(top(k), full(x(k), inflow[k])))
    above, through = [None] * NSEG, [None] * NSEG
    above[-1] = through[-1] = [zero] * 4
    for k in reversed(range(1, NSEG)):
        w = add(bottom(k), symm(q(k), inflow[k]))
        if k < NSEG - 1:
            w = add(w, full_t(x(k), through[k]))
        above[k - 1] = w
        through[k - 1] = full_t(factors[k], w)
    return below, above, through


def owner(*refs):
    parts, (tabs, _, maps_in), (*outs, maps_out), (recv, back) = (
        refs[:NSEG],
        refs[NSEG : NSEG + 3],
        refs[NSEG + 3 : -2],
        refs[-2:],
    )
    maps_out[...] = maps_in[...]
    from_partners(parts, recv, R1)

    def get(k, v):
        return recv[pl.ds(R1 * k + 6 * v, 8), :]

    def values(first, count):
        return lambda k: [get(k, first + e) for e in range(count)]

    def bottom_block(k):
        return look(tabs, T_P, 16, jnp.bitwise_and(get(k, 34).astype(I32), 127))

    below, above, _ = scan(bottom_block, values(0, 4), values(4, 4), values(8, 16), values(24, 10))
    none = jnp.full((6, 128), float(NONE), F32)
    for k in range(NSEG):
        rows = [v[:6] for v in below[k] + above[k]]
        rows.append(get(k + 1, 34)[:6] if k + 1 < NSEG else none)
        rows += [get(k - 1, 35 + e)[:6] if k > 0 else none for e in range(2)]
        for v, value in enumerate(rows + [none]):
            back[pl.ds(R2 * k + 6 * v, 6), :] = value
    to_partners(back, outs, R2)


def scan_split(*refs):
    chips, fields = refs[:NSEG], refs[NSEG : 2 * NSEG]
    lu, fixed, tabs, keep, give, every, maps, picked = refs[2 * NSEG :]
    me = lax.axis_index("gz_0")
    for d in range(NSEG):
        every[jnp.bitwise_xor(me, d)] = chips[d][...]
        maps[jnp.bitwise_xor(me, d)] = fields[d][...]
    low_half = half() == 0
    for lj in range(3):

        def values(ref, first, count):
            return lambda k: [ref[k, first + e, lj] for e in range(count)]

        def bottom_block(k):
            return look(tabs, T_P, 16, maps[k, 26, lj].astype(I32))

        found = scan(
            bottom_block, values(every, 0, 4), values(every, 4, 4), values(maps, 0, 16), values(maps, 16, 10)
        )
        for k in range(NSEG):
            for v, value in enumerate(found[0][k] + found[1][k] + found[2][k]):
                picked[k, v] = value
        mine = [picked[me, v] for v in range(12)]
        low, high = split_values(lu, fixed, tabs, lj, mine[:4], mine[4:8], mine[8:])
        for v in range(8):
            keep[v, lj] = jnp.where(low_half, low[v], high[v])
            give[v, lj] = jnp.where(low_half, high[v], low[v])


def make_apply(first):
    def apply(r, pb, sb, keep, got, first_keep, first_got, tabs, other, u, zlow, zup, near, far, dots, hscr, st):
        core = half()

        def get(n, v, own=keep, other=got):
            xi, lj = COLS[n]
            return jnp.where(core == xi, own[v, lj], other[v, lj])

        for n in range(6):
            for c in range(4):
                st[n, c] = get(n, c)

        def up(z, carry):
            for n, (xi, lj) in enumerate(COLS):
                rows, lanes = tile(xi, lj)
                g = full([pb[z, n, e] for e in range(16)], [st[n, c] for c in range(4)])
                g = add([r[z, c, rows, lanes] for c in range(4)], g)
                for c in range(4):
                    st[n, c] = g[c]
                h = symm([sb[z, n, e] for e in range(10)], g)
                for c in range(4):
                    hscr[z, n, c] = h[c]
            return carry

        lax.fori_loop(0, NZ, up, 0)
        zero = jnp.zeros((8, 128), F32)
        for n, (xi, lj) in enumerate(COLS):
            rows, lanes = tile(xi, lj)
            b = [get(n, 4 + c) for c in range(4)]
            t = full_t(look(tabs, T_P, 16, get(n, 8, first_keep, first_got).astype(I32)), b)
            for c in range(4):
                zup[c, rows, lanes] = b[c]
                st[n, c] = t[c]

        def down(s, carry):
            z = NZ - 1 - s
            ar, ao = carry
            for n, (xi, lj) in enumerate(COLS):
                rows, lanes = tile(xi, lj)
                w = [hscr[z, n, c] + st[n, c] for c in range(4)]
                for c in range(4):
                    u[z, c, rows, lanes] = w[c]
                ar = ar + fsum(w[c] * r[z, c, rows, lanes] for c in range(4))
                if not first:
                    ao = ao + fsum(w[c] * other[z, c, rows, lanes] for c in range(4))
                t = full_t([pb[z, n, e] for e in range(16)], w)
                for c in range(4):
                    st[n, c] = t[c]
            return ar, ao

        acc_r, acc_o = lax.fori_loop(0, NZ, down, (zero, zero))
        dots[0] = acc_r
        dots[1] = acc_o
        for n, (xi, lj) in enumerate(COLS):
            rows, lanes = tile(xi, lj)
            lay_id, mat_id = [get(n, 9 + e, first_keep, first_got).astype(I32) for e in range(2)]
            below = symm(look(tabs, T_S, 10, mat_id), [get(n, c) for c in range(4)])
            below = add(below, [st[n, c] for c in range(4)])
            pushed = symm(look(tabs, T_C, 10, lay_id), below)
            for c in range(4):
                zlow[c, rows, lanes] = pushed[c]

        even = xy_index() % 2 == 0

        def edges(z, carry):
            for c in range(4):
                first_row, last_row = u[z, c, pl.ds(0, 1), :], u[z, c, pl.ds(15, 1), :]
                near[z, pl.ds(c, 1), :] = jnp.where(even, last_row, first_row)
                far[z, pl.ds(c, 1), :] = jnp.where(even, first_row, last_row)
            return carry

        lax.fori_loop(0, NZ, edges, 0)

    return apply


def operator(u, kc, zlow, zup, out, dots, push):
    col = lax.broadcasted_iota(I32, (8, 384), 1)
    row = lax.broadcasted_iota(I32, (8, 384), 0)
    push[...] = zlow[...]

    def level(z, acc):
        for xi in range(2):
            rows = pl.ds(8 * xi, 8)
            side = []
            for c in range(4):
                here = u[z, c, rows, :]
                west = jnp.where(col == 0, 0.0, pltpu.roll(here, 1, 1))
                east = jnp.where(col == 383, 0.0, pltpu.roll(here, 383, 1))
                other = u[z, c, pl.ds(8 * (1 - xi), 8), :]
                down = pltpu.roll(here, 1, 0)
                upw = pltpu.roll(here, 7, 0)
                if xi == 0:
                    down = jnp.where(row == 0, 0.0, down)
                    upw = jnp.where(row == 7, pltpu.roll(other, 7, 0), upw)
                else:
                    down = jnp.where(row == 0, pltpu.roll(other, 1, 0), down)
                    upw = jnp.where(row == 7, 0.0, upw)
                side.append((west + east) + (down + upw))
            for lj in range(3):
                lanes = pl.ds(128 * lj, 128)
                v = [u[z, c, rows, lanes] for c in range(4)]
                nz = jnp.minimum(z + 1, NZ - 1)
                above = [
                    jnp.where(z == NZ - 1, zup[c, rows, lanes], u[nz, c, rows, lanes])
                    for c in range(4)
                ]
                n = 3 * xi + lj
                kv = symm([kc[z, n, e] for e in range(10)], v)
                cb = [kc[z, n, 10 + e] for e in range(10)]
                fa = symm(cb, above)
                fb = symm(cb, v)
                val = []
                for c in range(4):
                    near = side[c][:, 128 * lj : 128 * (lj + 1)]
                    val.append(kv[c] - near - fa[c] - push[c, rows, lanes])
                    out[z, c, rows, lanes] = val[c]
                    push[c, rows, lanes] = fb[c]
                acc = acc + fsum(val[c] * v[c] for c in range(4))
        return acc

    dots[0] = lax.fori_loop(0, NZ, level, jnp.zeros((8, 128), F32))


def edge_dot(near, far, own_near, own_far):
    index = xy_index()
    last = lax.axis_size("xy_0") * lax.axis_size("xy_1") - 1
    inside = (index > 0) & (index < last)
    outer = jnp.where(inside, far[...], 0.0) * own_far[...]
    return jnp.sum(near[...] * own_near[...] + outer, axis=0)


def halo_masks():
    row = lax.broadcasted_iota(I32, (8, 128), 0)
    index = xy_index()
    last = lax.axis_size("xy_0") * lax.axis_size("xy_1") - 1
    return index % 2 == 0, ((row == 0) & (index > 0), (row == 7) & (index < last))


def with_halo(part, near, far, z, c, xi, lj, masks):
    rows, lanes = tile(xi, lj)
    even, inside = masks
    a, b = near[z, pl.ds(c, 1), lanes], far[z, pl.ds(c, 1), lanes]
    edge = jnp.where(even, b, a) if xi == 0 else jnp.where(even, a, b)
    return part[z, c, rows, lanes] - jnp.where(inside[xi], edge, 0.0)


def second_sweep(part, near, far, pb, sb, image, keep, give, hscr, st):
    masks = halo_masks()
    zero = jnp.zeros((8, 128), F32)
    for n in range(6):
        for c in range(4):
            st[n, c] = zero

    def up(z, carry):
        for n, (xi, lj) in enumerate(COLS):
            rows, lanes = tile(xi, lj)
            blk = [pb[z, n, e] for e in range(16)]
            img = [with_halo(part, near, far, z, c, xi, lj, masks) for c in range(4)]
            for c in range(4):
                image[z, c, rows, lanes] = img[c]
            g = add(img, full(blk, [st[n, c] for c in range(4)]))
            for c in range(4):
                st[n, c] = g[c]
            h = symm([sb[z, n, e] for e in range(10)], g)
            for c in range(4):
                hscr[z, n, c] = h[c]
        return carry

    lax.fori_loop(0, NZ, up, 0)
    up_last = []
    for n in range(6):
        for c in range(4):
            up_last.append(st[n, c])
            st[n, c] = hscr[NZ - 1, n, c]

    def down(s, carry):
        z = NZ - 2 - s
        for n in range(6):
            t = full_t([pb[z + 1, n, e] for e in range(16)], [st[n, c] for c in range(4)])
            for c in range(4):
                st[n, c] = hscr[z, n, c] + t[c]
        return carry

    for core in range(2):

        @pl.when(half() == core)
        def _():
            for n, (xi, lj) in enumerate(COLS):
                for c in range(4):
                    (keep if xi == core else give)[c, lj] = up_last[4 * n + c]

    lax.fori_loop(0, NZ - 1, down, 0)
    for core in range(2):

        @pl.when(half() == core)
        def _():
            for n, (xi, lj) in enumerate(COLS):
                for c in range(4):
                    (keep if xi == core else give)[4 + c, lj] = st[n, c]


def last_dots(near, far, *refs):
    (near_w, far_w, nu, fu, own_nu, own_fu), (da, db, dc, dd, sums) = refs[:6], refs[6:]
    lane = lax.broadcasted_iota(I32, (1, 128), 1)
    line = jnp.zeros((1, 128), F32)
    curv0 = jnp.sum(dc[0]) - jnp.sum(edge_dot(nu, fu, own_nu, own_fu))
    curv1 = jnp.sum(dd[0]) - jnp.sum(edge_dot(near, far, near_w, far_w))
    for e, value in enumerate((jnp.sum(da[0]), curv0, jnp.sum(db[0]), jnp.sum(db[1]), curv1)):
        line = jnp.where(lane == e, value, line)
    sums[...] = jnp.broadcast_to(line[None], sums.shape)


def combine(sums, r, u, image, w, part, near, far, sol_hbm, res_hbm, sol, res, sems):
    tot = fsum([jnp.sum(sums[pl.ds(16 * k, 16)], axis=0) for k in range(8)])
    ru, ui, iw, rw, wy = [tot[:, e : e + 1] for e in range(5)]
    a0 = ru / ui
    fresh = ru - a0 * (rw + ui) + a0 * a0 * iw
    beta1 = 1.0 + fresh / ru
    curv = beta1 * beta1 * ui - beta1 * a0 * (iw + iw) + a0 * a0 * wy
    a1 = fresh / curv
    s0 = jnp.broadcast_to(a0 + a1 * beta1, (8, 128))
    s1 = jnp.broadcast_to(a1 * a0, (8, 128))
    masks = halo_masks()

    def copies(z):
        return [
            pltpu.make_async_copy(src.at[z], dst.at[z], sems.at[e, z])
            for e, (src, dst) in enumerate(((sol, sol_hbm), (res, res_hbm)))
        ]

    def level(z, carry):
        for xi, lj in COLS:
            rows, lanes = tile(xi, lj)
            for c in range(4):
                at = (z, c, rows, lanes)
                sol[at] = s0 * u[at] - s1 * w[at]
                y = with_halo(part, near, far, z, c, xi, lj, masks)
                res[at] = r[at] - s0 * image[at] + s1 * y
        for cp in copies(z):
            cp.start()
        return carry

    lax.fori_loop(0, NZ, level, 0)

    def finish(z, carry):
        for cp in copies(z):
            cp.wait()
        return carry

    lax.fori_loop(0, NZ, finish, 0)


def call(body, out, nargs, hbm=(), scratch=(), sems=(), limit=10, to_hbm=False):
    vm = pl.BlockSpec(memory_space=pltpu.VMEM)
    hb = pl.BlockSpec(memory_space=pltpu.HBM)
    return pl.pallas_call(
        body,
        out_shape=[s if hasattr(s, "dtype") else jax.ShapeDtypeStruct(s, F32) for s in out],
        in_specs=[hb if n in hbm else vm for n in range(nargs)],
        out_specs=[hb if to_hbm else vm for _ in out],
        scratch_shapes=[s if hasattr(s, "dtype") else pltpu.VMEM(s, F32) for s in scratch]
        + [pltpu.SemaphoreType.DMA(s) for s in sems],
        compiler_params=pltpu.CompilerParams(vmem_limit_bytes=limit * MIB),
    )


FIELD = (NZ, 4, 16, 384)
EDGE = (NZ, 4, 384)
PLANE = (4, 16, 384)
TABS = (NTAB, 8, 128)
SCR = ((NZ, 6, 4, 8, 128), (6, 4, 8, 128))
PB = (NZ, 6, 16, 8, 128)
SB = (NZ, 6, 10, 8, 128)
KC = (NZ, 6, 20, 8, 128)


def exchange(parts):
    count = lax.axis_size("gz_0")
    moved = [parts[0]]
    for d in range(1, len(parts)):
        moved.append(lax.ppermute(parts[d], "gz_0", [(i, i ^ d) for i in range(count)]))
    return moved


def blocks_of(per):
    return [(per, 128)] * NSEG


def swap(buf):
    return lax.ppermute(buf, "gz_1", [(0, 1), (1, 0)])


def part_of(count):
    return (count, 3, 8, 128)


def halo(near, far):
    count = lax.axis_size(XY)
    around = [((i + 1) % count, ((i ^ 1) + 1) % count) for i in range(count)]
    far = lax.ppermute(far, XY, around)
    near = lax.ppermute(near, XY, [(i, i ^ 1) for i in range(count)])
    return near, far


def apply_m(first, r, pb, sb, inflow, first_inflow, tabs, other):
    outs = (FIELD, PLANE, PLANE, EDGE, EDGE, (2, 8, 128))
    return call(make_apply(first), outs, 9, scratch=SCR)(
        r, pb, sb, *inflow, *first_inflow, tabs, other
    )


def operate(u, kc, zlow, zup):
    return call(operator, (FIELD, (1, 8, 128)), 4, scratch=(PLANE,))(u, kc, zlow, zup)


def per_device(load, mat, lay, stf, cpl, piv, fac):
    hbm_args = [load, mat, lay] + [jnp.transpose(t, (1, 2, 0)) for t in (fac, piv, stf, cpl)]
    hbm_args = [pltpu.with_memory_space_constraint(v, pltpu.HBM) for v in hbm_args]
    ids = [jax.ShapeDtypeStruct(v.shape, I32) for v in (mat, lay)]
    keep, give, tabs, load, mat, lay, pb = call(
        first_sweep,
        (part_of(37), part_of(37), TABS, FIELD, *ids, PB),
        7,
        hbm=range(7),
        scratch=[(6, 34, 8, 128)] + [pltpu.SMEM(v.shape, F32) for v in hbm_args[3:]],
        sems=((3, NZ // CHUNK), (4,)),
    )(*hbm_args)
    lu, maps, *send = call(
        make_merge(True),
        ((2, *part_of(37)), part_of(27), *blocks_of(R1)),
        3,
        scratch=((NSEG * R1, 128),),
    )(keep, swap(give), tabs)
    sent = exchange(send)
    sb, kc, token = call(expand, (SB, KC, (8, 128)), 4)(mat, lay, tabs, send[0])
    *back, maps = call(
        owner, (*blocks_of(R2), part_of(27)), NSEG + 3, scratch=((NSEG * R1, 128), (NSEG * R2, 128))
    )(*sent, tabs, token, maps)
    backs = exchange(back)
    all_maps = exchange([maps] * NSEG)
    keep, give = call(
        split, (part_of(11), part_of(11)), NSEG + 2, scratch=((NSEG * R2, 128),)
    )(*backs, lu, tabs)
    inflow1 = (keep, swap(give))
    u, zlow, zup, near_u, far_u, da = apply_m(True, load, pb, sb, inflow1, inflow1, tabs, load)
    edges_u = halo(near_u, far_u)
    part, dc = operate(u, kc, zlow, zup)
    image, keep, give = call(
        second_sweep, (FIELD, part_of(8), part_of(8)), 5, scratch=SCR
    )(part, *edges_u, pb, sb)
    lu2, chip = call(make_merge(False), ((2, *part_of(8)), part_of(8)), 4)(
        keep, swap(give), lu, tabs
    )
    keep, give = call(
        scan_split,
        (part_of(8), part_of(8)),
        2 * NSEG + 3,
        scratch=((NSEG, *part_of(8)), (NSEG, *part_of(27)), (NSEG, 12, 8, 128)),
    )(*exchange([chip] * NSEG), *all_maps, lu2, lu, tabs)
    w, zlow, zup, near_w, far_w, db = apply_m(
        False, image, pb, sb, (keep, swap(give)), inflow1, tabs, load
    )
    edges_w = halo(near_w, far_w)
    part, dd = operate(w, kc, zlow, zup)
    (sums,) = call(last_dots, ((128, 1, 128),), 12)(
        *edges_w, near_w, far_w, *edges_u, near_u, far_u, da, db, dc, dd
    )
    sums = lax.all_to_all(sums, ALL, 0, 0, tiled=True)
    return tuple(
        call(
            combine, (FIELD, FIELD), 8, scratch=(FIELD, FIELD), sems=((2, NZ),), to_hbm=True
        )(sums, load, u, image, w, part, *edges_w)
    )


def solution(mesh):
    finer = Mesh(mesh.devices.reshape(4, 2, 4, 4), ALL)
    return jax.shard_map(
        per_device,
        mesh=finer,
        in_specs=(P(GZ, None, XY, None), P(GZ, XY, None), P(GZ, XY, None), P(), P(), P(), P()),
        out_specs=(P(GZ, None, XY, None), P(GZ, None, XY, None)),
        check_vma=False,
    )
```
